768 devices in a mesh: tile: 24 (over z_lo, x), head: 32 (over z_hi, y, core).
Axes of the slice: x: 4, y: 8, z: 12 (z_hi: 2, z_lo: 6; z = z_hi * 6 + z_lo), core: 2. Of those that a mesh axis runs over, the one named last changes fastest.
Arguments:
- embedded: bfloat16 [24, 1024, 16, 64], P('tile', 'head'), may hold values from -6 to 6
- cotangent: bfloat16 [24, 1024, 16, 64], P('tile', 'head'), may hold values from -6 to 6
- weights: bfloat16 [1024, 4, 8, 128], P('head'), may hold values from -0.1875 to 0.1875
Outputs:
- attention: bfloat16 [24, 1024, 16, 64], P('tile', 'head')
- token_grads: float32 [24, 1024, 16, 64], P('tile', 'head')
- weight_grads: float32 [1024, 4, 8, 128], P('head')
The draws below stay inside these ranges and needn't reach their ends.
All inputs are finite; a program needn't handle non-finite values.
Results may differ from the reference program's by a relative error of at most 0.022.
Values may be sent and summed in bfloat16 or wider, within the bound.
No kernel may reach another device: no remote copies, remote signals or barrier semaphores. Data moves between devices by JAX's collectives and lax.ppermute only.
A program may use at most 32 MiB of HBM per device.

```python
import jax
import jax.numpy as jnp
from jax import lax

D = 1024
HEADS = 8
HEAD_DIM = 128
TILE_ROWS = 16
TILE_COLS = 16
RIM = 4
TILES_DEV = 4
STRIP = 64
GRID_ROWS = 12
GRID_COLS = 8
PAD_ROWS = 24
PAD_COLS = 24
TILE_TOKENS = 256
PAD_TOKENS = 576
N_TILE = 24


def shard_levels(key, dims, cuts, low, top_value):
    loudness = 1.0
    for axis_at, blocks in cuts:
        steps = jax.random.uniform(jax.random.fold_in(jax.random.fold_in(key, 6), axis_at), (blocks,), jnp.float32, low / len(cuts), top_value / len(cuts))
        loudness = loudness * jnp.repeat(jnp.exp(steps), dims[axis_at] // blocks).reshape((-1,) + (1,) * (len(dims) - 1 - axis_at))
    return loudness


def scatter_about(key, shape, width, bound, split=(), kind=jnp.bfloat16):
    result = jax.random.normal(key, shape, jnp.float32) * width
    if len(split) > 0:
        result = shard_levels(key, shape, split, -0.22, 0.18) * result
    return jnp.clip(result, min=-bound, max=bound).astype(kind)


def setup_inputs(seed: int = 0) -> dict:
    arg_keys = jax.random.split(jax.random.key(seed), 4)
    return {
        "embedded": scatter_about(arg_keys[0], (N_TILE, D, TILE_ROWS, STRIP), 1.0, 6.0, ((0, 24), (1, 32))),
        "cotangent": scatter_about(arg_keys[1], (N_TILE, D, TILE_ROWS, STRIP), 1.0, 6.0, ((0, 24), (1, 32))),
        "weights": scatter_about(arg_keys[2], (D, 4, HEADS, HEAD_DIM), D ** -0.5, 0.1875, ((0, 32),)),
    }


def to_picture(blocks):
    return blocks.reshape(GRID_ROWS, 2, D, TILE_ROWS, STRIP).transpose(0, 3, 1, 4, 2).reshape(GRID_ROWS * TILE_ROWS, 2 * STRIP, D)


def from_picture(picture):
    return picture.reshape(GRID_ROWS, TILE_ROWS, 2, STRIP, D).transpose(0, 2, 4, 1, 3).reshape(GRID_ROWS * 2, D, TILE_ROWS, STRIP)


def reference(embedded, cotangent, weights):
    score_scale = HEAD_DIM ** -0.5
    picture = to_picture(embedded)
    grad_picture = to_picture(cotangent)
    height = GRID_ROWS * TILE_ROWS
    breadth = GRID_COLS * TILE_COLS
    padded = jnp.pad(picture, ((RIM, RIM), (RIM, RIM), (0, 0)))
    wfull = weights.astype(jnp.float32)
    w_query = wfull[:, 0]
    w_key = wfull[:, 1]
    w_value = wfull[:, 2]
    w_out = wfull[:, 3]
    zero_index = jnp.zeros((), jnp.int32)

    def one_tile(state_pair, tile_index):
        grad_field, weight_acc = state_pair
        row_id = tile_index // GRID_COLS
        col_id = tile_index % GRID_COLS
        start_row = (row_id * TILE_ROWS).astype(jnp.int32)
        start_col = (col_id * TILE_COLS).astype(jnp.int32)
        window = lax.dynamic_slice(padded, (start_row, start_col, zero_index), (PAD_ROWS, PAD_COLS, D))
        grad_tile = lax.dynamic_slice(grad_picture, (start_row, start_col, zero_index), (TILE_ROWS, TILE_COLS, D))
        row_pos = start_row + jnp.arange(PAD_ROWS) - RIM
        col_pos = start_col + jnp.arange(PAD_COLS) - RIM
        key_valid = (((row_pos >= 0) & (row_pos < height))[:, None] & ((col_pos >= 0) & (col_pos < breadth))[None, :]).reshape(PAD_TOKENS)
        window_f = window.reshape(PAD_TOKENS, D).astype(jnp.float32)
        inner_f = window[RIM:RIM + TILE_ROWS, RIM:RIM + TILE_COLS].reshape(TILE_TOKENS, D).astype(jnp.float32)
        grad_f = grad_tile.reshape(TILE_TOKENS, D).astype(jnp.float32)
        queries = jnp.einsum('td,dhe->the', inner_f, w_query).astype(jnp.bfloat16).astype(jnp.float32)
        keys = jnp.einsum('pd,dhe->phe', window_f, w_key).astype(jnp.bfloat16).astype(jnp.float32)
        values = jnp.einsum('pd,dhe->phe', window_f, w_value).astype(jnp.bfloat16).astype(jnp.float32)
        scores = jnp.einsum('the,phe->htp', queries, keys) * score_scale
        scores = jnp.where(key_valid[None, None, :], scores, -jnp.inf)
        top_score = jnp.max(scores, axis=-1, keepdims=True)
        expo = jnp.exp(scores - top_score)
        probs = expo / jnp.sum(expo, axis=-1, keepdims=True)
        probs_low = probs.astype(jnp.bfloat16).astype(jnp.float32)
        attended = jnp.einsum('htp,phe->the', probs_low, values).astype(jnp.bfloat16).astype(jnp.float32)
        parts = jnp.einsum('the,dhe->htd', attended, w_out).astype(jnp.bfloat16)
        out_tile = jnp.sum(parts.astype(jnp.float32), axis=0).astype(jnp.bfloat16)
        d_attended = jnp.einsum('td,dhe->the', grad_f, w_out).astype(jnp.bfloat16).astype(jnp.float32)
        grad_out_w = jnp.einsum('td,the->dhe', grad_f, attended)
        d_probs = jnp.einsum('the,phe->htp', d_attended, values)
        d_scores = (probs * (d_probs - jnp.sum(d_probs * probs, axis=-1, keepdims=True)) * score_scale).astype(jnp.bfloat16).astype(jnp.float32)
        d_queries = jnp.einsum('htp,phe->the', d_scores, keys).astype(jnp.bfloat16).astype(jnp.float32)
        d_keys = jnp.einsum('htp,the->phe', d_scores, queries).astype(jnp.bfloat16).astype(jnp.float32)
        d_values = jnp.einsum('htp,the->phe', probs_low, d_attended).astype(jnp.bfloat16).astype(jnp.float32)
        grad_query_w = jnp.einsum('td,the->dhe', inner_f, d_queries)
        grad_key_w = jnp.einsum('pd,phe->dhe', window_f, d_keys)
        grad_value_w = jnp.einsum('pd,phe->dhe', window_f, d_values)
        d_window = jnp.einsum('phe,dhe->hpd', d_keys, w_key) + jnp.einsum('phe,dhe->hpd', d_values, w_value)
        d_inner = jnp.einsum('the,dhe->htd', d_queries, w_query)
        d_window = d_window.reshape(HEADS, PAD_ROWS, PAD_COLS, D).at[:, RIM:RIM + TILE_ROWS, RIM:RIM + TILE_COLS].add(d_inner.reshape(HEADS, TILE_ROWS, TILE_COLS, D))
        d_window = jnp.sum(d_window.astype(jnp.bfloat16).astype(jnp.float32), axis=0)
        current = lax.dynamic_slice(grad_field, (start_row, start_col, zero_index), (PAD_ROWS, PAD_COLS, D))
        grad_field = lax.dynamic_update_slice(grad_field, current + d_window, (start_row, start_col, zero_index))
        weight_term = jnp.stack([grad_query_w, grad_key_w, grad_value_w, grad_out_w], axis=1)
        tile_slot = col_id % TILES_DEV
        weight_acc = weight_acc.at[tile_slot].add(weight_term)
        return (grad_field, weight_acc), out_tile

    grad_start = jnp.zeros((height + 2 * RIM, breadth + 2 * RIM, D), jnp.float32)
    weight_start = jnp.zeros((TILES_DEV, D, 4, HEADS, HEAD_DIM), jnp.float32)
    (grad_field, weight_acc), out_tiles = lax.scan(one_tile, (grad_start, weight_start), jnp.arange(GRID_ROWS * GRID_COLS, dtype=jnp.int32))
    out_picture = out_tiles.reshape(GRID_ROWS, GRID_COLS, TILE_ROWS, TILE_COLS, D).transpose(0, 2, 1, 3, 4).reshape(height, breadth, D)
    attention = from_picture(out_picture)
    token_grads = from_picture(grad_field[RIM:RIM + height, RIM:RIM + breadth])
    rounded = lax.optimization_barrier(weight_acc.astype(jnp.bfloat16))
    weight_grads = jnp.sum(rounded.astype(jnp.float32), axis=0)
    return attention, token_grads, weight_grads
```

```python
import jax
import jax.numpy as jnp
from jax import lax
from jax.sharding import Mesh, PartitionSpec as P

D = 1024
HEADS = 8
HEAD_DIM = 128
TILE_ROWS = 16
TILE_COLS = 16
RIM = 4
PAD_ROWS = 24
PAD_COLS = 24
TILE_TOKENS = 256
PAD_TOKENS = 576
WIDTH = 32
ROWS_TOTAL = 192
COLS_TOTAL = 128

AXES = ("zl", "x", "zh", "y", "c")
SIZES = (6, 4, 2, 8, 2)

bf16 = jnp.bfloat16
f32 = jnp.float32

SWAP2 = [(0, 1), (1, 0)]


def right_pairs():
    pairs = []
    for x in range(4):
        for y in range(8):
            for c in range(2):
                col = (x % 2) * 4 + (y % 2) * 2 + c + 1
                if col < 8:
                    k = col % 4
                    to = (x - x % 2 + col // 4, y - y % 2 + k // 2, k % 2)
                    pairs.append((x * 16 + y * 2 + c, to[0] * 16 + to[1] * 2 + to[2]))
    return pairs


RIGHT = right_pairs()
LEFT = [(b, a) for a, b in RIGHT]
DOWN = [(t, t + 2) for t in range(22)]
UP = [(t + 2, t) for t in range(22)]


def to_right(v):
    return lax.ppermute(v, ("x", "y", "c"), RIGHT)


def to_left(v):
    return lax.ppermute(v, ("x", "y", "c"), LEFT)


def to_down(v):
    return lax.ppermute(v, ("zl", "x"), DOWN)


def to_up(v):
    return lax.ppermute(v, ("zl", "x"), UP)


def a2a(v, axes):
    return lax.all_to_all(v, axes, 0, 0, tiled=True)


def dot(a, b, da, db):
    return lax.dot_general(a, b, (((da,), (db,)), ((), ())), preferred_element_type=f32)


def split_tiles(block):
    return (
        block.reshape(WIDTH, TILE_ROWS, 2, 2, TILE_COLS)
        .transpose(2, 3, 0, 1, 4)
        .reshape(2, 2, WIDTH, TILE_TOKENS)
    )


def join_tiles(tiles):
    return (
        tiles.reshape(2, 2, WIDTH, TILE_ROWS, TILE_COLS)
        .transpose(2, 3, 1, 0, 4)
        .reshape(1, WIDTH, TILE_ROWS, 64)
    )


def local(embedded, cotangent, weights):
    score_scale = HEAD_DIM ** (-0.5)
    zl = lax.axis_index("zl")
    x = lax.axis_index("x")
    zh = lax.axis_index("zh")
    y = lax.axis_index("y")
    c = lax.axis_index("c")

    w_mine = lax.dynamic_index_in_dim(weights, x, 1, keepdims=False).transpose(1, 0, 2)
    w_keep = lax.dynamic_slice_in_dim(w_mine, zh * 4, 4, 0)
    w_give = lax.dynamic_slice_in_dim(w_mine, (1 - zh) * 4, 4, 0)
    w_got = lax.ppermute(w_give, "zh", SWAP2)
    w_rows = jnp.concatenate([w_keep, w_got], 1)
    w_send = jnp.broadcast_to(w_rows[:, None], (4, 2, 64, HEAD_DIM)).reshape(8, 64, HEAD_DIM)
    w_x = a2a(w_send, "y").reshape(512, HEAD_DIM)

    own = jnp.stack([split_tiles(embedded[0]), split_tiles(cotangent[0])], 2)
    other = lax.ppermute(own, "zh", SWAP2)
    both = jnp.stack([own, other], 3)
    both = both.transpose(1, 0, 2, 3, 4, 5)
    mine = a2a(both, "c")
    mine = mine.transpose(1, 2, 0, 3, 4, 5).reshape(1, 2, 2, 2, 64, TILE_TOKENS)
    t_send = jnp.broadcast_to(mine, (4, 2, 2, 2, 64, TILE_TOKENS)).reshape(8, 2, 2, 64, TILE_TOKENS)
    t_in = a2a(t_send, "y")
    t_in = t_in.transpose(1, 2, 0, 3, 4).reshape(2, D, TILE_TOKENS)
    tokens = t_in[0]
    grads = t_in[1]

    w_all = lax.all_gather(w_x, "x")
    w_all = lax.all_gather(w_all, "c")
    w_all = w_all.transpose(0, 2, 1, 3).reshape(D, 4 * HEAD_DIM)
    w_qkv = w_all[:, : 3 * HEAD_DIM]
    w_out = w_all[:, 3 * HEAD_DIM :]

    qkv = dot(tokens, w_qkv, 0, 0).astype(bf16)
    queries = qkv[:, :HEAD_DIM]
    kv = qkv[:, HEAD_DIM:].reshape(TILE_ROWS, TILE_COLS, 2 * HEAD_DIM)
    from_left = to_right(kv[:, TILE_COLS - RIM :])
    from_right = to_left(kv[:, :RIM])
    wide = jnp.concatenate([from_left, kv, from_right], 1)
    from_above = to_down(wide[TILE_ROWS - RIM :])
    from_below = to_up(wide[:RIM])
    window = jnp.concatenate([from_above, wide, from_below], 0).reshape(PAD_TOKENS, 2 * HEAD_DIM)
    keys = window[:, :HEAD_DIM]
    values = window[:, HEAD_DIM:]

    row_pos = (zl * 2 + x // 2) * TILE_ROWS + jnp.arange(PAD_ROWS) - RIM
    col_pos = ((x % 2) * 4 + (y % 2) * 2 + c) * TILE_COLS + jnp.arange(PAD_COLS) - RIM
    key_valid = (
        ((row_pos >= 0) & (row_pos < ROWS_TOTAL))[:, None]
        & ((col_pos >= 0) & (col_pos < COLS_TOTAL))[None, :]
    ).reshape(PAD_TOKENS)

    scores = dot(queries, keys, 1, 1) * score_scale
    scores = jnp.where(key_valid[None, :], scores, -jnp.inf)
    top_score = jnp.max(scores, axis=-1, keepdims=True)
    expo = jnp.exp(scores - top_score)
    probs = expo / jnp.sum(expo, axis=-1, keepdims=True)
    probs_low = probs.astype(bf16)
    attended = dot(probs_low, values, 1, 0).astype(bf16)
    part = dot(w_out, attended, 1, 1).astype(bf16)
    d_attended = dot(grads, w_out, 0, 0).astype(bf16)
    d_probs = dot(d_attended, values, 1, 1)
    d_scores = (
        probs * (d_probs - jnp.sum(d_probs * probs, axis=-1, keepdims=True)) * score_scale
    ).astype(bf16)
    d_queries = dot(d_scores, keys, 1, 0).astype(bf16)
    d_keys = dot(d_scores, queries, 0, 0)
    d_values = dot(probs_low, d_attended, 0, 0)
    d_window = jnp.concatenate([d_keys, d_values], 1).astype(bf16)
    d_window = d_window.reshape(PAD_ROWS, PAD_COLS, 2 * HEAD_DIM)
    back_below = to_up(d_window[:RIM])
    back_above = to_down(d_window[RIM + TILE_ROWS :])
    d_mid = d_window[RIM : RIM + TILE_ROWS].astype(f32)
    d_mid = (
        d_mid
        + jnp.pad(back_below.astype(f32), ((TILE_ROWS - RIM, 0), (0, 0), (0, 0)))
        + jnp.pad(back_above.astype(f32), ((0, TILE_ROWS - RIM), (0, 0), (0, 0)))
    )
    back_right = to_left(d_mid[:, :RIM].astype(bf16))
    back_left = to_right(d_mid[:, RIM + TILE_COLS :].astype(bf16))
    d_kv = (
        d_mid[:, RIM : RIM + TILE_COLS]
        + jnp.pad(back_right.astype(f32), ((0, 0), (TILE_COLS - RIM, 0), (0, 0)))
        + jnp.pad(back_left.astype(f32), ((0, 0), (0, TILE_COLS - RIM), (0, 0)))
    )
    d_kv = d_kv.astype(bf16).reshape(TILE_TOKENS, 2 * HEAD_DIM)
    d_qkv = jnp.concatenate([d_queries, d_kv], 1)

    dw = jnp.concatenate([dot(tokens, d_qkv, 1, 0), dot(grads, attended, 1, 0)], 1).astype(bf16)
    dw = dw.reshape(2, 512, 4, HEAD_DIM).transpose(2, 0, 1, 3).reshape(8, 512, HEAD_DIM)
    dw = jnp.sum(a2a(dw, ("x", "c")).astype(f32), 0).astype(bf16)
    dw = a2a(dw.reshape(8, 64, HEAD_DIM), "y")
    dw = jnp.sum(dw.reshape(4, 2, 64, HEAD_DIM).astype(f32), 1).astype(bf16)
    dw = dw.reshape(4, 2, WIDTH, HEAD_DIM)
    dw_near, dw_far = dw[:, 0], dw[:, 1]
    first = zh == 0
    dw = jnp.stack([jnp.where(first, dw_near, dw_far), jnp.where(first, dw_far, dw_near)])
    dw = jnp.broadcast_to(dw[None], (6, 2, 4, WIDTH, HEAD_DIM)).reshape(12, 4, WIDTH, HEAD_DIM)
    dw = a2a(dw, ("zl", "zh")).reshape(6, HEADS, WIDTH, HEAD_DIM)
    dw = jnp.sum(dw.astype(f32), 0).astype(bf16)
    dw = lax.all_gather(dw, "x")
    weight_grads = dw.transpose(2, 0, 1, 3).astype(f32)

    d_tokens = dot(w_qkv, d_qkv, 1, 1).astype(bf16)
    back = jnp.stack([part, d_tokens]).reshape(2, 2, 8, 2, WIDTH, TILE_TOKENS)
    back = back.transpose(2, 0, 1, 3, 4, 5)
    back = a2a(back, "y").reshape(4, 2, 2, 2, 2, WIDTH, TILE_TOKENS).astype(f32)
    back = jnp.sum(back, 0)
    far = lax.ppermute(back[:, :, :, 1].astype(bf16), "zh", SWAP2)
    back = back[:, :, :, 0] + far.astype(f32)
    out = a2a(back[:, 0].astype(bf16).transpose(1, 0, 2, 3), "c")
    grad = a2a(back[:, 1].transpose(1, 0, 2, 3), "c")
    return join_tiles(out), join_tiles(grad), weight_grads


def solution(mesh):
    inner = Mesh(mesh.devices.reshape(SIZES), AXES)
    strips = P(("zl", "x"), ("zh", "y", "c"), None, None)
    rows = P(("zh", "y", "c"), None, None, None)
    return jax.shard_map(
        local,
        mesh=inner,
        in_specs=(strips, strips, rows),
        out_specs=(strips, strips, rows),
        check_vma=False,
    )
```

```python
import jax
import jax.numpy as jnp
from jax import lax
from jax.sharding import Mesh, PartitionSpec as P


D = 1024
HEAD_DIM = 128
TILE_ROWS = 16
TILE_COLS = 16
RIM = 4
PAD_ROWS = 24
PAD_COLS = 24
TILE_TOKENS = 256
PAD_TOKENS = 576
WIDTH = 32
ROWS_TOTAL = 192
COLS_TOTAL = 128

AXES = ("zl", "x", "zh", "y", "c")
SIZES = (6, 4, 2, 8, 2)

bf16 = jnp.bfloat16
f32 = jnp.float32


def right_pairs():
    pairs = []
    for x in range(4):
        for y in range(8):
            for c in range(2):
                col = (x % 2) * 4 + (y % 2) * 2 + c + 1
                if col < 8:
                    k = col % 4
                    to = (x - x % 2 + col // 4, y - y % 2 + k // 2, k % 2)
                    pairs.append((x * 16 + y * 2 + c, to[0] * 16 + to[1] * 2 + to[2]))
    return pairs


RIGHT = right_pairs()
LEFT = [(b, a) for a, b in RIGHT]
DOWN = [(t, t + 2) for t in range(22)]
UP = [(t + 2, t) for t in range(22)]


def to_right(v):
    return lax.ppermute(v, ("x", "y", "c"), RIGHT)


def to_left(v):
    return lax.ppermute(v, ("x", "y", "c"), LEFT)


def to_down(v):
    return lax.ppermute(v, ("zl", "x"), DOWN)


def to_up(v):
    return lax.ppermute(v, ("zl", "x"), UP)


def a2a(v, axes):
    return lax.all_to_all(v, axes, 0, 0, tiled=True)


def dot(a, b, da, db):
    return lax.dot_general(a, b, (((da,), (db,)), ((), ())), preferred_element_type=f32)


def shift(v, axis, count, step, by):
    size = lax.axis_size(axis)
    ring = count * step
    pairs = []
    for i in range(size):
        base = i - i % ring
        pairs.append((i, base + (i % ring - by * step) % ring))
    return lax.ppermute(v, axis, pairs)


def swap(v, axis):
    return lax.ppermute(v, axis, [(i, i ^ 1) for i in range(lax.axis_size(axis))])


def swap_diag(v):
    return lax.ppermute(v, ("zh", "y", "c"), [(i, (i ^ 1) ^ 16) for i in range(32)])


def pick(v, index, axis=0):
    return lax.dynamic_index_in_dim(v, index, axis, keepdims=False)


def unroll(parts, me):
    return lax.dynamic_slice_in_dim(jnp.stack(parts + parts), (4 - me) % 4, 4, 0)


def in_order(mine, other, bit):
    first = bit == 0
    return jnp.where(first, mine, other), jnp.where(first, other, mine)


def split_tiles(block):
    return (
        block.reshape(WIDTH, TILE_ROWS, 2, 2, TILE_COLS)
        .transpose(2, 3, 0, 1, 4)
        .reshape(2, 2, WIDTH, TILE_TOKENS)
    )


def join_tiles(tiles):
    return (
        tiles.reshape(2, 2, WIDTH, TILE_ROWS, TILE_COLS)
        .transpose(2, 3, 1, 0, 4)
        .reshape(1, WIDTH, TILE_ROWS, 64)
    )


def work(embedded, cotangent, weights):
    score_scale = HEAD_DIM ** (-0.5)
    zl = lax.axis_index("zl")
    x = lax.axis_index("x")
    zh = lax.axis_index("zh")
    y = lax.axis_index("y")
    c = lax.axis_index("c")

    y2 = y // 2
    b = y % 2

    w_mine = pick(weights, x, 1).transpose(1, 0, 2)
    w_keep = lax.dynamic_slice_in_dim(w_mine, zh * 4, 4, 0)
    w_give = lax.dynamic_slice_in_dim(w_mine, (1 - zh) * 4, 4, 0)
    w_zh = swap(w_give, "zh")
    w_zc = swap_diag(w_give)
    w_c = swap(w_keep, "c")
    w_rows = jnp.stack([w_keep, w_zh, w_c, w_zc], 1).reshape(4, 128, HEAD_DIM)
    w_near = [pick(w_rows, y2)] + [
        shift(pick(w_rows, (y2 - s) % 4), "y", 4, 2, s) for s in (1, 2, 3)
    ]
    w_near = unroll(w_near, y2)
    w_even, w_odd = in_order(w_near, swap(w_near, "y"), b)
    w_x = jnp.stack([w_even, w_odd], 1).reshape(D, HEAD_DIM)

    def gather_tiles(block):
        own = split_tiles(block)
        keep = pick(own, c, 1)
        give = pick(own, 1 - c, 1)
        mine = jnp.stack([keep, swap(keep, "zh"), swap(give, "c"), swap_diag(give)], 1)
        mine = mine.reshape(1, 2, 128, TILE_TOKENS)
        send = jnp.broadcast_to(mine, (4, 2, 128, TILE_TOKENS)).reshape(8, 128, TILE_TOKENS)
        return a2a(send, "y").reshape(D, TILE_TOKENS)

    tokens = gather_tiles(embedded[0])
    grads = gather_tiles(cotangent[0])

    w_list = jnp.stack([w_x] + [shift(w_x, "x", 4, 1, s) for s in (1, 2, 3)])
    w_qkv = jnp.concatenate([pick(w_list, (m - x) % 4) for m in range(3)], 1)
    w_out = pick(w_list, (3 - x) % 4)

    qkv = dot(tokens, w_qkv, 0, 0).astype(bf16)
    queries = qkv[:, :HEAD_DIM]
    kv = qkv[:, HEAD_DIM:].reshape(TILE_ROWS, TILE_COLS, 2 * HEAD_DIM)
    from_left = to_right(kv[:, TILE_COLS - RIM :])
    from_right = to_left(kv[:, :RIM])
    wide = jnp.concatenate([from_left, kv, from_right], 1)
    from_above = to_down(wide[TILE_ROWS - RIM :])
    from_below = to_up(wide[:RIM])
    window = jnp.concatenate([from_above, wide, from_below], 0).reshape(PAD_TOKENS, 2 * HEAD_DIM)
    keys = window[:, :HEAD_DIM]
    values = window[:, HEAD_DIM:]

    row_pos = (zl * 2 + x // 2) * TILE_ROWS + jnp.arange(PAD_ROWS) - RIM
    col_pos = ((x % 2) * 4 + (y % 2) * 2 + c) * TILE_COLS + jnp.arange(PAD_COLS) - RIM
    key_valid = (
        ((row_pos >= 0) & (row_pos < ROWS_TOTAL))[:, None]
        & ((col_pos >= 0) & (col_pos < COLS_TOTAL))[None, :]
    ).reshape(PAD_TOKENS)

    scores = dot(queries, keys, 1, 1) * score_scale
    scores = jnp.where(key_valid[None, :], scores, -jnp.inf)
    top_score = jnp.max(scores, axis=-1, keepdims=True)
    expo = jnp.exp(scores - top_score)
    probs = expo / jnp.sum(expo, axis=-1, keepdims=True)
    probs_low = probs.astype(bf16)
    attended = dot(probs_low, values, 1, 0).astype(bf16)
    part = dot(w_out, attended, 1, 1).astype(bf16)
    d_attended = dot(grads, w_out, 0, 0).astype(bf16)
    d_probs = dot(d_attended, values, 1, 1)
    d_scores = (
        probs * (d_probs - jnp.sum(d_probs * probs, axis=-1, keepdims=True)) * score_scale
    ).astype(bf16)
    d_queries = dot(d_scores, keys, 1, 0).astype(bf16)
    d_keys = dot(d_scores, queries, 0, 0)
    d_values = dot(probs_low, d_attended, 0, 0)
    d_window = jnp.concatenate([d_keys, d_values], 1).astype(bf16)
    d_window = d_window.reshape(PAD_ROWS, PAD_COLS, 2 * HEAD_DIM)
    back_below = to_up(d_window[:RIM])
    back_above = to_down(d_window[RIM + TILE_ROWS :])
    d_mid = d_window[RIM : RIM + TILE_ROWS].astype(f32)
    d_mid = (
        d_mid
        + jnp.pad(back_below.astype(f32), ((TILE_ROWS - RIM, 0), (0, 0), (0, 0)))
        + jnp.pad(back_above.astype(f32), ((0, TILE_ROWS - RIM), (0, 0), (0, 0)))
    )
    back_right = to_left(d_mid[:, :RIM].astype(bf16))
    back_left = to_right(d_mid[:, RIM + TILE_COLS :].astype(bf16))
    d_kv = (
        d_mid[:, RIM : RIM + TILE_COLS]
        + jnp.pad(back_right.astype(f32), ((0, 0), (TILE_COLS - RIM, 0), (0, 0)))
        + jnp.pad(back_left.astype(f32), ((0, 0), (0, TILE_COLS - RIM), (0, 0)))
    )
    d_kv = d_kv.astype(bf16).reshape(TILE_TOKENS, 2 * HEAD_DIM)
    d_qkv = jnp.concatenate([d_queries, d_kv], 1)

    d_tokens = dot(w_qkv, d_qkv, 1, 1).astype(bf16)
    back = jnp.stack([part.reshape(8, 128, TILE_TOKENS), d_tokens.reshape(8, 128, TILE_TOKENS)], 1)
    back = a2a(back, "y")
    back = back.reshape(4, 2, 2, 2, 2, WIDTH, TILE_TOKENS).astype(f32)
    back = jnp.sum(back, 0)
    low = back.astype(bf16)
    own_tile = back[:, :, 0, 0] + swap(low[:, :, 0, 1], "zh").astype(f32)
    other_tile = swap(back[:, :, 1, 0], "c") + swap_diag(low[:, :, 1, 1]).astype(f32)
    left, right = in_order(own_tile, other_tile, c)
    back = jnp.stack([left, right])
    attention = join_tiles(back[:, :, 0].astype(bf16))
    token_grads = join_tiles(back[:, :, 1])

    def core_sum(mats):
        mats = mats.reshape(8, 2, 64, -1)
        return mats[:, 0] + swap(mats[:, 1].astype(bf16), "c").astype(f32)

    dw_q = core_sum(dot(tokens, d_queries, 1, 0))
    dw_o = core_sum(dot(grads, attended, 1, 0))
    dw_kv = core_sum(dot(tokens, d_kv, 1, 0))
    dw = jnp.stack([dw_q, dw_kv[:, :, :HEAD_DIM], dw_kv[:, :, HEAD_DIM:], dw_o])
    dw_low = dw.astype(bf16)
    total = pick(dw, x)
    for s in (1, 2, 3):
        got = shift(pick(dw_low, (x - s) % 4), "x", 4, 1, s)
        total = total + got.astype(f32)
    total = total.reshape(4, 2, 64, HEAD_DIM)
    total = pick(total, b, 1) + swap(pick(total.astype(bf16), 1 - b, 1), "y").astype(f32)
    low = total.astype(bf16)
    heads = [pick(low, y2)] + [shift(pick(low, (y2 - s) % 4), "y", 4, 2, s) for s in (1, 2, 3)]
    heads = unroll(heads, y2).reshape(4, 2, WIDTH, HEAD_DIM)
    low_heads, high_heads = in_order(heads[:, 0], swap(heads[:, 1], "zh"), zh)
    total = jnp.concatenate([low_heads, high_heads])
    total = (total.astype(f32) + swap(total, "zl").astype(f32)).astype(bf16)
    total = (
        total.astype(f32)
        + shift(total, "zl", 3, 2, 1).astype(f32)
        + shift(total, "zl", 3, 2, 2).astype(f32)
    ).astype(bf16)
    total = unroll([total] + [shift(total, "x", 4, 1, s) for s in (1, 2, 3)], x)
    weight_grads = total.transpose(2, 0, 1, 3).astype(f32)
    return attention, token_grads, weight_grads


def solution(mesh):
    inner = Mesh(mesh.devices.reshape(SIZES), AXES)
    strips = P(("zl", "x"), ("zh", "y", "c"), None, None)
    rows = P(("zh", "y", "c"), None, None, None)
    return jax.shard_map(
        work,
        mesh=inner,
        in_specs=(strips, strips, rows),
        out_specs=(strips, strips, rows),
        check_vma=False,
    )
```

```python
import jax
import jax.numpy as jnp
from jax import lax
from jax.sharding import Mesh, PartitionSpec as P


D = 1024
HEADS = 8
HEAD_DIM = 128
TILE_ROWS = 16
TILE_COLS = 16
RIM = 4
PAD_ROWS = 24
PAD_COLS = 24
TILE_TOKENS = 256
PAD_TOKENS = 576
WIDTH = 32
ROWS_TOTAL = 192
COLS_TOTAL = 128

AXES = ("zl", "x", "zh", "y", "c")
SIZES = (6, 4, 2, 8, 2)

bf16 = jnp.bfloat16
f32 = jnp.float32


def right_pairs():
    pairs = []
    for x in range(4):
        for y in range(8):
            for c in range(2):
                col = (x % 2) * 4 + (y % 2) * 2 + c + 1
                if col < 8:
                    k = col % 4
                    to = (x - x % 2 + col // 4, y - y % 2 + k // 2, k % 2)
                    pairs.append((x * 16 + y * 2 + c, to[0] * 16 + to[1] * 2 + to[2]))
    return pairs


RIGHT = right_pairs()
LEFT = [(b, a) for a, b in RIGHT]
DOWN = [(t, t + 2) for t in range(22)]
UP = [(t + 2, t) for t in range(22)]


def to_right(v):
    return lax.ppermute(v, ("x", "y", "c"), RIGHT)


def to_left(v):
    return lax.ppermute(v, ("x", "y", "c"), LEFT)


def to_down(v):
    return lax.ppermute(v, ("zl", "x"), DOWN)


def to_up(v):
    return lax.ppermute(v, ("zl", "x"), UP)


def a2a(v, axes):
    return lax.all_to_all(v, axes, 0, 0, tiled=True)


def dot(a, b, da, db):
    return lax.dot_general(a, b, (((da,), (db,)), ((), ())), preferred_element_type=f32)


def shift(v, axis, count, step, by):
    size = lax.axis_size(axis)
    ring = count * step
    pairs = []
    for i in range(size):
        base = i - i % ring
        pairs.append((i, base + (i % ring - by * step) % ring))
    return lax.ppermute(v, axis, pairs)


def swap(v, axis):
    return lax.ppermute(v, axis, [(i, i ^ 1) for i in range(lax.axis_size(axis))])


def pick(v, index, axis=0):
    return lax.dynamic_index_in_dim(v, index, axis, keepdims=False)


def unroll(parts, me):
    return lax.dynamic_slice_in_dim(jnp.stack(parts + parts), (4 - me) % 4, 4, 0)


def in_order(mine, other, bit):
    first = bit == 0
    return jnp.where(first, mine, other), jnp.where(first, other, mine)


def split_tiles(block):
    return (
        block.reshape(WIDTH, 2, 8, 2, 2, TILE_COLS)
        .transpose(3, 4, 1, 0, 2, 5)
        .reshape(2, 2, 2, WIDTH, 128)
    )


def join_tiles(tiles):
    return (
        tiles.reshape(2, 2, 2, WIDTH, 8, TILE_COLS)
        .transpose(3, 2, 4, 1, 0, 5)
        .reshape(1, WIDTH, TILE_ROWS, 64)
    )


def work(embedded, cotangent, weights):
    score_scale = HEAD_DIM ** (-0.5)
    zl = lax.axis_index("zl")
    x = lax.axis_index("x")
    zh = lax.axis_index("zh")
    y = lax.axis_index("y")
    c = lax.axis_index("c")

    w_mine = pick(weights, x, 1).transpose(1, 0, 2)
    w_keep = lax.dynamic_slice_in_dim(w_mine, zh * 4, 4, 0)
    w_give = lax.dynamic_slice_in_dim(w_mine, (1 - zh) * 4, 4, 0)
    tiles = jnp.concatenate([split_tiles(embedded[0]), split_tiles(cotangent[0])], 2)
    mine = jnp.concatenate([tiles.reshape(16, WIDTH, 128), w_give])
    got = swap(mine, "zh")
    pairs = jnp.stack([tiles, got[:16].reshape(2, 2, 4, WIDTH, 128)], 3)
    t_keep = pick(pairs, c, 1)
    t_give = pick(pairs, 1 - c, 1)
    w_keep = jnp.stack([w_keep, got[16:]], 1)
    mine = jnp.concatenate([t_give.reshape(16, WIDTH, 128), w_keep.reshape(8, WIDTH, 128)])
    got = swap(mine, "c")
    t_mine = jnp.stack([t_keep, got[:16].reshape(2, 4, 2, WIDTH, 128)], 2)
    t_mine = t_mine.reshape(2, 4, 128, 128)
    w_mine = jnp.stack([w_keep, got[16:].reshape(4, 2, WIDTH, 128)], 1).reshape(4, 128, 128)
    t_mine = t_mine.transpose(0, 2, 1, 3).reshape(1, 2, 128, 512)
    send = jnp.concatenate(
        [
            jnp.broadcast_to(t_mine, (4, 2, 128, 512)),
            jnp.broadcast_to(w_mine[:, None], (4, 2, 128, 128)),
        ],
        3,
    )
    got = a2a(send.reshape(8, 128, 640), "y").reshape(D, 640)
    tokens = got[:, :TILE_TOKENS]
    grads = got[:, TILE_TOKENS : 2 * TILE_TOKENS]
    w_x = got[:, 2 * TILE_TOKENS :]

    w_list = jnp.stack([w_x] + [shift(w_x, "x", 4, 1, s) for s in (1, 2, 3)])
    w_qkv = jnp.concatenate([pick(w_list, (m - x) % 4) for m in range(3)], 1)
    w_out = pick(w_list, (3 - x) % 4)

    qkv = dot(tokens, w_qkv, 0, 0).astype(bf16)
    queries = qkv[:, :HEAD_DIM]
    kv = qkv[:, HEAD_DIM:].reshape(TILE_ROWS, TILE_COLS, 2 * HEAD_DIM)
    from_left = to_right(kv[:, TILE_COLS - RIM :])
    from_right = to_left(kv[:, :RIM])
    wide = jnp.concatenate([from_left, kv, from_right], 1)
    from_above = to_down(wide[TILE_ROWS - RIM :])
    from_below = to_up(wide[:RIM])
    window = jnp.concatenate([from_above, wide, from_below], 0).reshape(PAD_TOKENS, 2 * HEAD_DIM)
    keys = window[:, :HEAD_DIM]
    values = window[:, HEAD_DIM:]

    row_pos = (zl * 2 + x // 2) * TILE_ROWS + jnp.arange(PAD_ROWS) - RIM
    col_pos = ((x % 2) * 4 + (y % 2) * 2 + c) * TILE_COLS + jnp.arange(PAD_COLS) - RIM
    key_valid = (
        ((row_pos >= 0) & (row_pos < ROWS_TOTAL))[:, None]
        & ((col_pos >= 0) & (col_pos < COLS_TOTAL))[None, :]
    ).reshape(PAD_TOKENS)

    scores = dot(queries, keys, 1, 1) * score_scale
    scores = jnp.where(key_valid[None, :], scores, -jnp.inf)
    top_score = jnp.max(scores, axis=-1, keepdims=True)
    expo = jnp.exp(scores - top_score)
    probs = expo / jnp.sum(expo, axis=-1, keepdims=True)
    probs_low = probs.astype(bf16)
    attended = dot(probs_low, values, 1, 0).astype(bf16)
    part = dot(w_out, attended, 1, 1).astype(bf16)
    d_attended = dot(grads, w_out, 0, 0).astype(bf16)
    d_probs = dot(d_attended, values, 1, 1)
    d_scores = (
        probs * (d_probs - jnp.sum(d_probs * probs, axis=-1, keepdims=True)) * score_scale
    ).astype(bf16)
    d_queries = dot(d_scores, keys, 1, 0).astype(bf16)
    d_keys = dot(d_scores, queries, 0, 0)
    d_values = dot(probs_low, d_attended, 0, 0)
    d_window = jnp.concatenate([d_keys, d_values], 1).astype(bf16)
    d_window = d_window.reshape(PAD_ROWS, PAD_COLS, 2 * HEAD_DIM)
    back_below = to_up(d_window[:RIM])
    back_above = to_down(d_window[RIM + TILE_ROWS :])
    d_mid = d_window[RIM : RIM + TILE_ROWS].astype(f32)
    d_mid = (
        d_mid
        + jnp.pad(back_below.astype(f32), ((TILE_ROWS - RIM, 0), (0, 0), (0, 0)))
        + jnp.pad(back_above.astype(f32), ((0, TILE_ROWS - RIM), (0, 0), (0, 0)))
    )
    back_right = to_left(d_mid[:, :RIM].astype(bf16))
    back_left = to_right(d_mid[:, RIM + TILE_COLS :].astype(bf16))
    d_kv = (
        d_mid[:, RIM : RIM + TILE_COLS]
        + jnp.pad(back_right.astype(f32), ((0, 0), (TILE_COLS - RIM, 0), (0, 0)))
        + jnp.pad(back_left.astype(f32), ((0, 0), (0, TILE_COLS - RIM), (0, 0)))
    )
    d_kv = d_kv.astype(bf16).reshape(TILE_TOKENS, 2 * HEAD_DIM)
    d_qkv = jnp.concatenate([d_queries, d_kv], 1)

    d_tokens = dot(w_qkv, d_qkv, 1, 1).astype(bf16)
    dw_kv = dot(tokens, d_kv, 1, 0)
    dw = jnp.stack(
        [
            dot(tokens, d_queries, 1, 0),
            dw_kv[:, :HEAD_DIM],
            dw_kv[:, HEAD_DIM:],
            dot(grads, attended, 1, 0),
        ]
    ).astype(bf16)
    total = pick(dw, x).astype(f32)
    for s in (1, 2, 3):
        total = total + shift(pick(dw, (x - s) % 4), "x", 4, 1, s).astype(f32)
    send = jnp.concatenate([part, d_tokens, total.astype(bf16)], 1).reshape(8, 128, 640)
    got = a2a(send, "y").reshape(4, 2, 128, 640)
    back = jnp.sum(got[..., :512].astype(f32), 0)
    back = back.reshape(2, 2, 64, 4, 128).transpose(1, 0, 3, 2, 4)
    dw = jnp.sum(got[..., 512:].astype(f32), 1).reshape(4, 2, 64, 128)
    give = jnp.concatenate([back[1].reshape(8, 64, 128), dw[:, 1]]).astype(bf16)
    got = swap(give, "c")
    dw = (dw[:, 0] + got[8:].astype(f32)).astype(bf16).reshape(4, 2, WIDTH, 128)
    dw = jnp.stack(in_order(dw[:, 0], dw[:, 1], zh))
    dw = jnp.broadcast_to(dw, (6, 2, 4, WIDTH, 128)).reshape(12, 4, WIDTH, 128)
    dw = a2a(dw, ("zl", "zh"))
    total = jnp.sum(dw.reshape(6, HEADS, WIDTH, 128).astype(f32), 0).astype(bf16)

    back = jnp.stack([back[0], got[:8].reshape(2, 4, 64, 128).astype(f32)])
    back = back.reshape(2, 2, 4, 2, WIDTH, 128)
    far = swap(back[:, :, :, 1].astype(bf16), "zh")
    back = back[:, :, :, 0] + far.astype(f32)
    back = jnp.stack(in_order(back[0], back[1], c))
    attention = join_tiles(back[:, :, :2].astype(bf16))
    token_grads = join_tiles(back[:, :, 2:])

    total = unroll([total] + [shift(total, "x", 4, 1, s) for s in (1, 2, 3)], x)
    weight_grads = total.transpose(2, 0, 1, 3).astype(f32)
    return attention, token_grads, weight_grads


def solution(mesh):
    inner = Mesh(mesh.devices.reshape(SIZES), AXES)
    strips = P(("zl", "x"), ("zh", "y", "c"), None, None)
    rows = P(("zh", "y", "c"), None, None, None)
    return jax.shard_map(
        work,
        mesh=inner,
        in_specs=(strips, strips, rows),
        out_specs=(strips, strips, rows),
        check_vma=False,
    )
```

```python
import jax
import jax.numpy as jnp
from jax import lax
from jax.sharding import Mesh, PartitionSpec as P


D = 1024
HEADS = 8
HEAD_DIM = 128
TILE_ROWS = 16
TILE_COLS = 16
RIM = 4
PAD_ROWS = 24
PAD_COLS = 24
TILE_TOKENS = 256
PAD_TOKENS = 576
WIDTH = 32
ROWS_TOTAL = 192
COLS_TOTAL = 128

AXES = ("zl", "x", "zh", "y", "c")
SIZES = (6, 4, 2, 8, 2)

bf16 = jnp.bfloat16
f32 = jnp.float32


def right_pairs():
    pairs = []
    for x in range(4):
        for y in range(8):
            for c in range(2):
                col = (x % 2) * 4 + (y % 2) * 2 + c + 1
                if col < 8:
                    k = col % 4
                    to = (x - x % 2 + col // 4, y - y % 2 + k // 2, k % 2)
                    pairs.append((x * 16 + y * 2 + c, to[0] * 16 + to[1] * 2 + to[2]))
    return pairs


RIGHT = right_pairs()
LEFT = [(b, a) for a, b in RIGHT]
DOWN = [(t, t + 2) for t in range(22)]
UP = [(t + 2, t) for t in range(22)]


def to_right(v):
    return lax.ppermute(v, ("x", "y", "c"), RIGHT)


def to_left(v):
    return lax.ppermute(v, ("x", "y", "c"), LEFT)


def to_down(v):
    return lax.ppermute(v, ("zl", "x"), DOWN)


def to_up(v):
    return lax.ppermute(v, ("zl", "x"), UP)


def a2a(v, axes):
    return lax.all_to_all(v, axes, 0, 0, tiled=True)


def dot(a, b, da, db):
    return lax.dot_general(a, b, (((da,), (db,)), ((), ())), preferred_element_type=f32)


def shift(v, axis, count, step, by):
    size = lax.axis_size(axis)
    ring = count * step
    pairs = []
    for i in range(size):
        base = i - i % ring
        pairs.append((i, base + (i % ring - by * step) % ring))
    return lax.ppermute(v, axis, pairs)


def swap(v, axis):
    return lax.ppermute(v, axis, [(i, i ^ 1) for i in range(lax.axis_size(axis))])


def pick(v, index, axis=0):
    return lax.dynamic_index_in_dim(v, index, axis, keepdims=False)


def unroll(parts, me):
    return lax.dynamic_slice_in_dim(jnp.stack(parts + parts), (4 - me) % 4, 4, 0)


def in_order(mine, other, bit):
    first = bit == 0
    return jnp.where(first, mine, other), jnp.where(first, other, mine)


def split_tiles(block):
    return (
        block.reshape(WIDTH, 2, 8, 2, 2, TILE_COLS)
        .transpose(3, 4, 1, 0, 2, 5)
        .reshape(2, 2, 2, WIDTH, 128)
    )


def join_tiles(tiles):
    return (
        tiles.reshape(2, 2, 2, WIDTH, 8, TILE_COLS)
        .transpose(3, 2, 4, 1, 0, 5)
        .reshape(1, WIDTH, TILE_ROWS, 64)
    )


def work(embedded, cotangent, weights):
    score_scale = HEAD_DIM ** (-0.5)
    zl = lax.axis_index("zl")
    x = lax.axis_index("x")
    zh = lax.axis_index("zh")
    y = lax.axis_index("y")
    c = lax.axis_index("c")

    w_mine = pick(weights, x, 1).transpose(1, 0, 2)
    w_keep = lax.dynamic_slice_in_dim(w_mine, zh * 4, 4, 0)
    w_give = lax.dynamic_slice_in_dim(w_mine, (1 - zh) * 4, 4, 0)
    tiles = jnp.concatenate([split_tiles(embedded[0]), split_tiles(cotangent[0])], 2)
    mine = jnp.concatenate([tiles.reshape(16, WIDTH, 128), w_give])
    got = swap(mine, "zh")
    pairs = jnp.stack([tiles, got[:16].reshape(2, 2, 4, WIDTH, 128)], 3)
    t_keep = pick(pairs, c, 1)
    t_give = pick(pairs, 1 - c, 1)
    w_keep = jnp.stack([w_keep, got[16:]], 1)
    mine = jnp.concatenate([t_give.reshape(16, WIDTH, 128), w_keep.reshape(8, WIDTH, 128)])
    got = swap(mine, "c")
    t_mine = jnp.stack([t_keep, got[:16].reshape(2, 4, 2, WIDTH, 128)], 2)
    t_mine = t_mine.reshape(2, 4, 128, 128)
    w_mine = jnp.stack([w_keep, got[16:].reshape(4, 2, WIDTH, 128)], 1).reshape(4, 128, 128)
    t_mine = t_mine.transpose(0, 2, 1, 3)

    def gather(v, lead):
        send = jnp.broadcast_to(v, lead + v.shape[2:]).reshape(8, 128, -1)
        return a2a(send, "y").reshape(D, -1)

    w_x = gather(w_mine[:, None], (4, 2))
    tokens = gather(t_mine[None, :, :, :2].reshape(1, 2, 128, TILE_TOKENS), (4, 2))
    grads = gather(t_mine[None, :, :, 2:].reshape(1, 2, 128, TILE_TOKENS), (4, 2))
    w_list = jnp.stack([w_x] + [shift(w_x, "x", 4, 1, s) for s in (1, 2, 3)])
    w_qkv = jnp.concatenate([pick(w_list, (m - x) % 4) for m in range(3)], 1)
    w_out = pick(w_list, (3 - x) % 4)

    qkv = dot(tokens, w_qkv, 0, 0).astype(bf16)
    queries = qkv[:, :HEAD_DIM]
    kv = qkv[:, HEAD_DIM:].reshape(TILE_ROWS, TILE_COLS, 2 * HEAD_DIM)
    from_left = to_right(kv[:, TILE_COLS - RIM :])
    from_right = to_left(kv[:, :RIM])
    wide = jnp.concatenate([from_left, kv, from_right], 1)
    from_above = to_down(wide[TILE_ROWS - RIM :])
    from_below = to_up(wide[:RIM])
    window = jnp.concatenate([from_above, wide, from_below], 0).reshape(PAD_TOKENS, 2 * HEAD_DIM)
    keys = window[:, :HEAD_DIM]
    values = window[:, HEAD_DIM:]

    row_pos = (zl * 2 + x // 2) * TILE_ROWS + jnp.arange(PAD_ROWS) - RIM
    col_pos = ((x % 2) * 4 + (y % 2) * 2 + c) * TILE_COLS + jnp.arange(PAD_COLS) - RIM
    key_valid = (
        ((row_pos >= 0) & (row_pos < ROWS_TOTAL))[:, None]
        & ((col_pos >= 0) & (col_pos < COLS_TOTAL))[None, :]
    ).reshape(PAD_TOKENS)

    scores = dot(queries, keys, 1, 1) * score_scale
    scores = jnp.where(key_valid[None, :], scores, -jnp.inf)
    top_score = jnp.max(scores, axis=-1, keepdims=True)
    expo = jnp.exp(scores - top_score)
    probs = expo / jnp.sum(expo, axis=-1, keepdims=True)
    probs_low = probs.astype(bf16)
    attended = dot(probs_low, values, 1, 0).astype(bf16)
    part = dot(w_out, attended, 1, 1).astype(bf16)
    d_attended = dot(grads, w_out, 0, 0).astype(bf16)
    d_probs = dot(d_attended, values, 1, 1)
    d_scores = (
        probs * (d_probs - jnp.sum(d_probs * probs, axis=-1, keepdims=True)) * score_scale
    ).astype(bf16)
    d_queries = dot(d_scores, keys, 1, 0).astype(bf16)
    d_keys = dot(d_scores, queries, 0, 0)
    d_values = dot(probs_low, d_attended, 0, 0)
    d_window = jnp.concatenate([d_keys, d_values], 1).astype(bf16)
    d_window = d_window.reshape(PAD_ROWS, PAD_COLS, 2 * HEAD_DIM)
    back_below = to_up(d_window[:RIM])
    back_above = to_down(d_window[RIM + TILE_ROWS :])
    d_mid = d_window[RIM : RIM + TILE_ROWS].astype(f32)
    d_mid = (
        d_mid
        + jnp.pad(back_below.astype(f32), ((TILE_ROWS - RIM, 0), (0, 0), (0, 0)))
        + jnp.pad(back_above.astype(f32), ((0, TILE_ROWS - RIM), (0, 0), (0, 0)))
    )
    back_right = to_left(d_mid[:, :RIM].astype(bf16))
    back_left = to_right(d_mid[:, RIM + TILE_COLS :].astype(bf16))
    d_kv = (
        d_mid[:, RIM : RIM + TILE_COLS]
        + jnp.pad(back_right.astype(f32), ((0, 0), (TILE_COLS - RIM, 0), (0, 0)))
        + jnp.pad(back_left.astype(f32), ((0, 0), (0, TILE_COLS - RIM), (0, 0)))
    )
    d_kv = d_kv.astype(bf16).reshape(TILE_TOKENS, 2 * HEAD_DIM)
    d_qkv = jnp.concatenate([d_queries, d_kv], 1)

    d_tokens = dot(w_qkv, d_qkv, 1, 1).astype(bf16)
    dw_kv = dot(tokens, d_kv, 1, 0)
    dw = jnp.stack(
        [
            dot(tokens, d_queries, 1, 0),
            dw_kv[:, :HEAD_DIM],
            dw_kv[:, HEAD_DIM:],
            dot(grads, attended, 1, 0),
        ]
    ).astype(bf16)
    total = pick(dw, x).astype(f32)
    for s in (1, 2, 3):
        got = shift(pick(dw, (x - s) % 4), "x", 4, 1, s)
        total = total + got.astype(f32)
    send = jnp.concatenate([part, d_tokens], 1).reshape(8, 128, 512)
    got = a2a(send, "y").reshape(4, 2, 128, 512)
    back = jnp.sum(got.astype(f32), 0)
    back = back.reshape(2, 2, 64, 4, 128).transpose(1, 0, 3, 2, 4)
    back_c = swap(back[1].astype(bf16), "c")
    got = a2a(total.astype(bf16).reshape(8, 128, 128), "y")
    dw = jnp.sum(got.reshape(4, 2, 128, 128).astype(f32), 1)
    dw = dw.reshape(4, 2, 64, 128)
    got = swap(dw[:, 1].astype(bf16), "c")
    dw = (dw[:, 0] + got.astype(f32)).astype(bf16).reshape(4, 2, WIDTH, 128)
    dw = jnp.stack(in_order(dw[:, 0], dw[:, 1], zh))
    dw = jnp.broadcast_to(dw, (6, 2, 4, WIDTH, 128)).reshape(12, 4, WIDTH, 128)
    dw = a2a(dw, ("zl", "zh"))
    total = jnp.sum(dw.reshape(6, HEADS, WIDTH, 128).astype(f32), 0).astype(bf16)

    back = jnp.stack([back[0], back_c.astype(f32)])
    back = back.reshape(2, 2, 4, 2, WIDTH, 128)
    far = swap(back[:, :, :, 1].astype(bf16), "zh")
    back = back[:, :, :, 0] + far.astype(f32)
    back = jnp.stack(in_order(back[0], back[1], c))
    attention = join_tiles(back[:, :, :2].astype(bf16))
    token_grads = join_tiles(back[:, :, 2:])

    total = unroll([total] + [shift(total, "x", 4, 1, s) for s in (1, 2, 3)], x)
    weight_grads = total.transpose(2, 0, 1, 3).astype(f32)
    return attention, token_grads, weight_grads


def solution(mesh):
    inner = Mesh(mesh.devices.reshape(SIZES), AXES)
    strips = P(("zl", "x"), ("zh", "y", "c"), None, None)
    rows = P(("zh", "y", "c"), None, None, None)
    return jax.shard_map(
        work,
        mesh=inner,
        in_specs=(strips, strips, rows),
        out_specs=(strips, strips, rows),
        check_vma=False,
    )
```

```python
import jax
import jax.numpy as jnp
from jax import lax
from jax.sharding import Mesh, PartitionSpec as P


D = 1024
HEADS = 8
HEAD_DIM = 128
TILE_ROWS = 16
TILE_COLS = 16
RIM = 4
PAD_ROWS = 24
PAD_COLS = 24
TILE_TOKENS = 256
PAD_TOKENS = 576
WIDTH = 32
ROWS_TOTAL = 192
COLS_TOTAL = 128

AXES = ("zl", "x", "zh", "y", "c")
SIZES = (6, 4, 2, 8, 2)

bf16 = jnp.bfloat16
f32 = jnp.float32


def right_pairs():
    pairs = []
    for x in range(4):
        for y in range(8):
            for c in range(2):
                col = (x % 2) * 4 + (y % 2) * 2 + c + 1
                if col < 8:
                    k = col % 4
                    to = (x - x % 2 + col // 4, y - y % 2 + k // 2, k % 2)
                    pairs.append((x * 16 + y * 2 + c, to[0] * 16 + to[1] * 2 + to[2]))
    return pairs


RIGHT = right_pairs()
LEFT = [(b, a) for a, b in RIGHT]
DOWN = [(t, t + 2) for t in range(22)]
UP = [(t + 2, t) for t in range(22)]
SWAP_X2 = [(i, i ^ 2) for i in range(4)]


def to_right(v):
    return lax.ppermute(v, ("x", "y", "c"), RIGHT)


def to_left(v):
    return lax.ppermute(v, ("x", "y", "c"), LEFT)


def to_down(v):
    return lax.ppermute(v, ("zl", "x"), DOWN)


def to_up(v):
    return lax.ppermute(v, ("zl", "x"), UP)


def a2a(v, axes):
    return lax.all_to_all(v, axes, 0, 0, tiled=True)


def dot(a, b, da, db):
    return lax.dot_general(a, b, (((da,), (db,)), ((), ())), preferred_element_type=f32)


def shift(v, axis, count, step, by):
    size = lax.axis_size(axis)
    ring = count * step
    pairs = []
    for i in range(size):
        base = i - i % ring
        pairs.append((i, base + (i % ring - by * step) % ring))
    return lax.ppermute(v, axis, pairs)


def swap(v, axis):
    return lax.ppermute(v, axis, [(i, i ^ 1) for i in range(lax.axis_size(axis))])


def pick(v, index, axis=0):
    return lax.dynamic_index_in_dim(v, index, axis, keepdims=False)


def in_order(mine, other, bit):
    first = bit == 0
    return jnp.where(first, mine, other), jnp.where(first, other, mine)


def split_tiles(block):
    return (
        block.reshape(WIDTH, 2, 8, 2, 2, TILE_COLS)
        .transpose(3, 4, 1, 0, 2, 5)
        .reshape(2, 2, 2, WIDTH, 128)
    )


def join_tiles(tiles):
    return (
        tiles.reshape(2, 2, 2, WIDTH, 8, TILE_COLS)
        .transpose(3, 2, 4, 1, 0, 5)
        .reshape(1, WIDTH, TILE_ROWS, 64)
    )


def work(embedded, cotangent, weights):
    score_scale = HEAD_DIM ** (-0.5)
    zl = lax.axis_index("zl")
    x = lax.axis_index("x")
    zh = lax.axis_index("zh")
    y = lax.axis_index("y")
    c = lax.axis_index("c")

    w_mine = pick(weights, x, 1).transpose(1, 0, 2)
    w_keep = lax.dynamic_slice_in_dim(w_mine, zh * 4, 4, 0)
    w_give = lax.dynamic_slice_in_dim(w_mine, (1 - zh) * 4, 4, 0)
    tiles = jnp.concatenate([split_tiles(embedded[0]), split_tiles(cotangent[0])], 2)
    mine = jnp.concatenate([tiles.reshape(16, WIDTH, 128), w_give])
    got = swap(mine, "zh")
    pairs = jnp.stack([tiles, got[:16].reshape(2, 2, 4, WIDTH, 128)], 3)
    t_keep = pick(pairs, c, 1)
    t_give = pick(pairs, 1 - c, 1)
    w_keep = jnp.stack([w_keep, got[16:]], 1)
    mine = jnp.concatenate([t_give.reshape(16, WIDTH, 128), w_keep.reshape(8, WIDTH, 128)])
    got = swap(mine, "c")
    t_mine = jnp.stack([t_keep, got[:16].reshape(2, 4, 2, WIDTH, 128)], 2)
    t_mine = t_mine.reshape(2, 4, 128, 128)
    w_mine = jnp.stack([w_keep, got[16:].reshape(4, 2, WIDTH, 128)], 1).reshape(4, 128, 128)
    t_mine = t_mine.transpose(0, 2, 1, 3)

    def gather(v, lead):
        send = jnp.broadcast_to(v, lead + v.shape[2:]).reshape(8, 128, -1)
        return a2a(send, "y").reshape(D, -1)

    w_x = gather(w_mine[:, None], (4, 2))
    both = gather(t_mine[None].reshape(1, 2, 128, 2 * TILE_TOKENS), (4, 2))
    tokens, grads = both[:, :TILE_TOKENS], both[:, TILE_TOKENS:]
    w_list = jnp.stack([w_x] + [shift(w_x, "x", 4, 1, s) for s in (1, 2, 3)])
    w_qkv = jnp.concatenate([pick(w_list, (m - x) % 4) for m in range(3)], 1)
    w_out = pick(w_list, (3 - x) % 4)

    qkv = dot(tokens, w_qkv, 0, 0).astype(bf16)
    queries = qkv[:, :HEAD_DIM]
    kv = qkv[:, HEAD_DIM:].reshape(TILE_ROWS, TILE_COLS, 2 * HEAD_DIM)
    from_left = to_right(kv[:, TILE_COLS - RIM :])
    from_right = to_left(kv[:, :RIM])
    wide = jnp.concatenate([from_left, kv, from_right], 1)
    from_above = to_down(wide[TILE_ROWS - RIM :])
    from_below = to_up(wide[:RIM])
    window = jnp.concatenate([from_above, wide, from_below], 0).reshape(PAD_TOKENS, 2 * HEAD_DIM)
    keys = window[:, :HEAD_DIM]
    values = window[:, HEAD_DIM:]

    row_pos = (zl * 2 + x // 2) * TILE_ROWS + jnp.arange(PAD_ROWS) - RIM
    col_pos = ((x % 2) * 4 + (y % 2) * 2 + c) * TILE_COLS + jnp.arange(PAD_COLS) - RIM
    key_valid = (
        ((row_pos >= 0) & (row_pos < ROWS_TOTAL))[:, None]
        & ((col_pos >= 0) & (col_pos < COLS_TOTAL))[None, :]
    ).reshape(PAD_TOKENS)

    scores = dot(queries, keys, 1, 1) * score_scale
    scores = jnp.where(key_valid[None, :], scores, -jnp.inf)
    top_score = jnp.max(scores, axis=-1, keepdims=True)
    expo = jnp.exp(scores - top_score)
    probs = expo / jnp.sum(expo, axis=-1, keepdims=True)
    probs_low = probs.astype(bf16)
    attended = dot(probs_low, values, 1, 0).astype(bf16)
    part = dot(w_out, attended, 1, 1).astype(bf16)
    d_attended = dot(grads, w_out, 0, 0).astype(bf16)
    d_probs = dot(d_attended, values, 1, 1)
    d_scores = (
        probs * (d_probs - jnp.sum(d_probs * probs, axis=-1, keepdims=True)) * score_scale
    ).astype(bf16)
    d_queries = dot(d_scores, keys, 1, 0).astype(bf16)
    d_keys = dot(d_scores, queries, 0, 0)
    d_values = dot(probs_low, d_attended, 0, 0)
    d_window = jnp.concatenate([d_keys, d_values], 1).astype(bf16)
    d_window = d_window.reshape(PAD_ROWS, PAD_COLS, 2 * HEAD_DIM)
    back_below = to_up(d_window[:RIM])
    back_above = to_down(d_window[RIM + TILE_ROWS :])
    d_mid = d_window[RIM : RIM + TILE_ROWS].astype(f32)
    d_mid = (
        d_mid
        + jnp.pad(back_below.astype(f32), ((TILE_ROWS - RIM, 0), (0, 0), (0, 0)))
        + jnp.pad(back_above.astype(f32), ((0, TILE_ROWS - RIM), (0, 0), (0, 0)))
    )
    back_right = to_left(d_mid[:, :RIM].astype(bf16))
    back_left = to_right(d_mid[:, RIM + TILE_COLS :].astype(bf16))
    d_kv = (
        d_mid[:, RIM : RIM + TILE_COLS]
        + jnp.pad(back_right.astype(f32), ((0, 0), (TILE_COLS - RIM, 0), (0, 0)))
        + jnp.pad(back_left.astype(f32), ((0, 0), (0, TILE_COLS - RIM), (0, 0)))
    )
    d_kv = d_kv.astype(bf16).reshape(TILE_TOKENS, 2 * HEAD_DIM)
    d_qkv = jnp.concatenate([d_queries, d_kv], 1)

    d_tokens = dot(w_qkv, d_qkv, 1, 1).astype(bf16)
    dw_kv = dot(tokens, d_kv, 1, 0)
    dw = jnp.stack(
        [
            dot(tokens, d_queries, 1, 0),
            dw_kv[:, :HEAD_DIM],
            dw_kv[:, HEAD_DIM:],
            dot(grads, attended, 1, 0),
        ]
    ).astype(bf16)
    total = pick(dw, x).astype(f32)
    for s in (1, 2, 3):
        got = shift(pick(dw, (x - s) % 4), "x", 4, 1, s)
        total = total + got.astype(f32)
    send = jnp.concatenate([part, d_tokens], 1).reshape(8, 128, 512)
    got = a2a(send, "y").reshape(4, 2, 128, 512)
    back = jnp.sum(got.astype(f32), 0)
    back = back.reshape(2, 2, 2, WIDTH, 4, 128).transpose(2, 1, 0, 4, 3, 5)
    far = swap(back[1].astype(bf16), "zh")
    back = back[0] + far.astype(f32)
    other = swap(back[1], "c")
    back = jnp.stack(in_order(back[0], other, c))
    attention = join_tiles(back[:, :, :2].astype(bf16))
    token_grads = join_tiles(back[:, :, 2:])

    total = total.reshape(8, 2, 64, 128)
    got = swap(total[:, 1].astype(bf16), "c")
    total = (total[:, 0] + got.astype(f32)).astype(bf16).reshape(8, 2, WIDTH, 128)
    got = swap(total[:, 1], "zh")
    total = jnp.stack(in_order(total[:, 0], got, zh), 1)
    total = a2a(total, "y")
    total = jnp.sum(total.reshape(4, 2, 2, WIDTH, 128).astype(f32), 1).astype(bf16)
    total = total.transpose(1, 0, 2, 3).reshape(1, HEADS, WIDTH, 128)
    total = jnp.broadcast_to(total, (6, HEADS, WIDTH, 128))
    total = a2a(total, "zl")
    total = jnp.sum(total.astype(f32), 0).astype(bf16)
    total = jnp.stack(in_order(total, swap(total, "x"), x % 2))
    total = jnp.concatenate(in_order(total, lax.ppermute(total, "x", SWAP_X2), x // 2))
    weight_grads = total.transpose(2, 0, 1, 3).astype(f32)
    return attention, token_grads, weight_grads


def solution(mesh):
    inner = Mesh(mesh.devices.reshape(SIZES), AXES)
    strips = P(("zl", "x"), ("zh", "y", "c"), None, None)
    rows = P(("zh", "y", "c"), None, None, None)
    return jax.shard_map(
        work,
        mesh=inner,
        in_specs=(strips, strips, rows),
        out_specs=(strips, strips, rows),
        check_vma=False,
    )
```

```python
import jax
import jax.numpy as jnp
from jax import lax
from jax.sharding import Mesh, PartitionSpec as P


D = 1024
HEADS = 8
HEAD_DIM = 128
TILE_ROWS = 16
TILE_COLS = 16
RIM = 4
PAD_ROWS = 24
PAD_COLS = 24
TILE_TOKENS = 256
PAD_TOKENS = 576
WIDTH = 32
ROWS_TOTAL = 192
COLS_TOTAL = 128

AXES = ("zl", "x", "zh", "y", "c")
SIZES = (6, 4, 2, 8, 2)

bf16 = jnp.bfloat16
f32 = jnp.float32


def right_pairs():
    pairs = []
    for x in range(4):
        for y in range(8):
            for c in range(2):
                col = (x % 2) * 4 + (y % 2) * 2 + c + 1
                if col < 8:
                    k = col % 4
                    to = (x - x % 2 + col // 4, y - y % 2 + k // 2, k % 2)
                    pairs.append((x * 16 + y * 2 + c, to[0] * 16 + to[1] * 2 + to[2]))
    return pairs


RIGHT = right_pairs()
LEFT = [(b, a) for a, b in RIGHT]
DOWN = [(t, t + 2) for t in range(22)]
UP = [(t + 2, t) for t in range(22)]
SWAP_X2 = [(i, i ^ 2) for i in range(4)]


def to_right(v):
    return lax.ppermute(v, ("x", "y", "c"), RIGHT)


def to_left(v):
    return lax.ppermute(v, ("x", "y", "c"), LEFT)


def to_down(v):
    return lax.ppermute(v, ("zl", "x"), DOWN)


def to_up(v):
    return lax.ppermute(v, ("zl", "x"), UP)


def a2a(v, axes):
    return lax.all_to_all(v, axes, 0, 0, tiled=True)


def dot(a, b, da, db):
    return lax.dot_general(a, b, (((da,), (db,)), ((), ())), preferred_element_type=f32)


def shift(v, axis, count, step, by):
    size = lax.axis_size(axis)
    ring = count * step
    pairs = []
    for i in range(size):
        base = i - i % ring
        pairs.append((i, base + (i % ring - by * step) % ring))
    return lax.ppermute(v, axis, pairs)


def swap(v, axis):
    return lax.ppermute(v, axis, [(i, i ^ 1) for i in range(lax.axis_size(axis))])


def pick(v, index, axis=0):
    return lax.dynamic_index_in_dim(v, index, axis, keepdims=False)


def in_order(mine, other, bit):
    first = bit == 0
    return jnp.where(first, mine, other), jnp.where(first, other, mine)


def split_tiles(block):
    return (
        block.reshape(WIDTH, 2, 8, 2, 2, TILE_COLS)
        .transpose(3, 4, 1, 0, 2, 5)
        .reshape(2, 2, 2, WIDTH, 128)
    )


def join_tiles(tiles):
    return (
        tiles.reshape(2, 2, 2, WIDTH, 8, TILE_COLS)
        .transpose(3, 2, 4, 1, 0, 5)
        .reshape(1, WIDTH, TILE_ROWS, 64)
    )


def work(embedded, cotangent, weights):
    score_scale = HEAD_DIM ** (-0.5)
    zl = lax.axis_index("zl")
    x = lax.axis_index("x")
    zh = lax.axis_index("zh")
    y = lax.axis_index("y")
    c = lax.axis_index("c")

    w_mine = pick(weights, x, 1).reshape(WIDTH, 2, 4, HEAD_DIM).transpose(2, 1, 0, 3)
    w_send = jnp.broadcast_to(w_mine[:, None], (4, 2, 2, WIDTH, HEAD_DIM))
    w_in = a2a(w_send.reshape(8, 2, WIDTH, HEAD_DIM), "y")

    tiles = jnp.concatenate([split_tiles(embedded[0]), split_tiles(cotangent[0])], 2)
    got = swap(tiles, "zh")
    pairs = jnp.stack([tiles, got], 3)
    t_keep = pick(pairs, c, 1)
    t_give = pick(pairs, 1 - c, 1)
    mine = jnp.concatenate([t_give.reshape(16, WIDTH, 128), w_in.reshape(16, WIDTH, 128)])
    got = swap(mine, "c")
    t_mine = jnp.stack([t_keep, got[:16].reshape(2, 4, 2, WIDTH, 128)], 2)
    t_mine = t_mine.reshape(2, 4, 128, 128).transpose(0, 2, 1, 3)
    send = jnp.broadcast_to(t_mine.reshape(1, 2, 128, 512), (4, 2, 128, 512))
    both = a2a(send.reshape(8, 128, 512), "y").reshape(D, 512)
    tokens, grads = both[:, :TILE_TOKENS], both[:, TILE_TOKENS:]

    w_both = jnp.stack([w_in, got[16:].reshape(8, 2, WIDTH, HEAD_DIM)], 2)
    w_far = swap(pick(w_both, 1 - zh, 1), "zh")
    w_x = jnp.stack([pick(w_both, zh, 1), w_far], 2).reshape(D, HEAD_DIM)
    w_list = jnp.stack([w_x] + [shift(w_x, "x", 4, 1, s) for s in (1, 2, 3)])
    w_qkv = jnp.concatenate([pick(w_list, (m - x) % 4) for m in range(3)], 1)
    w_out = pick(w_list, (3 - x) % 4)

    qkv = dot(tokens, w_qkv, 0, 0).astype(bf16)
    queries = qkv[:, :HEAD_DIM]
    kv = qkv[:, HEAD_DIM:].reshape(TILE_ROWS, TILE_COLS, 2 * HEAD_DIM)
    from_left = to_right(kv[:, TILE_COLS - RIM :])
    from_right = to_left(kv[:, :RIM])
    wide = jnp.concatenate([from_left, kv, from_right], 1)
    from_above = to_down(wide[TILE_ROWS - RIM :])
    from_below = to_up(wide[:RIM])
    window = jnp.concatenate([from_above, wide, from_below], 0).reshape(PAD_TOKENS, 2 * HEAD_DIM)
    keys = window[:, :HEAD_DIM]
    values = window[:, HEAD_DIM:]

    row_pos = (zl * 2 + x // 2) * TILE_ROWS + jnp.arange(PAD_ROWS) - RIM
    col_pos = ((x % 2) * 4 + (y % 2) * 2 + c) * TILE_COLS + jnp.arange(PAD_COLS) - RIM
    key_valid = (
        ((row_pos >= 0) & (row_pos < ROWS_TOTAL))[:, None]
        & ((col_pos >= 0) & (col_pos < COLS_TOTAL))[None, :]
    ).reshape(PAD_TOKENS)

    scores = dot(queries, keys, 1, 1) * score_scale
    scores = jnp.where(key_valid[None, :], scores, -jnp.inf)
    top_score = jnp.max(scores, axis=-1, keepdims=True)
    expo = jnp.exp(scores - top_score)
    probs = expo / jnp.sum(expo, axis=-1, keepdims=True)
    probs_low = probs.astype(bf16)
    attended = dot(probs_low, values, 1, 0).astype(bf16)
    part = dot(w_out, attended, 1, 1).astype(bf16)
    d_attended = dot(grads, w_out, 0, 0).astype(bf16)
    d_probs = dot(d_attended, values, 1, 1)
    d_scores = (
        probs * (d_probs - jnp.sum(d_probs * probs, axis=-1, keepdims=True)) * score_scale
    ).astype(bf16)
    d_queries = dot(d_scores, keys, 1, 0).astype(bf16)
    d_keys = dot(d_scores, queries, 0, 0)
    d_values = dot(probs_low, d_attended, 0, 0)
    d_window = jnp.concatenate([d_keys, d_values], 1).astype(bf16)
    d_window = d_window.reshape(PAD_ROWS, PAD_COLS, 2 * HEAD_DIM)
    back_below = to_up(d_window[:RIM])
    back_above = to_down(d_window[RIM + TILE_ROWS :])
    d_mid = d_window[RIM : RIM + TILE_ROWS].astype(f32)
    d_mid = (
        d_mid
        + jnp.pad(back_below.astype(f32), ((TILE_ROWS - RIM, 0), (0, 0), (0, 0)))
        + jnp.pad(back_above.astype(f32), ((0, TILE_ROWS - RIM), (0, 0), (0, 0)))
    )
    back_right = to_left(d_mid[:, :RIM].astype(bf16))
    back_left = to_right(d_mid[:, RIM + TILE_COLS :].astype(bf16))
    d_kv = (
        d_mid[:, RIM : RIM + TILE_COLS]
        + jnp.pad(back_right.astype(f32), ((0, 0), (TILE_COLS - RIM, 0), (0, 0)))
        + jnp.pad(back_left.astype(f32), ((0, 0), (0, TILE_COLS - RIM), (0, 0)))
    )
    d_kv = d_kv.astype(bf16).reshape(TILE_TOKENS, 2 * HEAD_DIM)
    d_qkv = jnp.concatenate([d_queries, d_kv], 1)

    d_tokens = dot(w_qkv, d_qkv, 1, 1).astype(bf16)
    dw_kv = dot(tokens, d_kv, 1, 0)
    dw = jnp.stack(
        [
            dot(tokens, d_queries, 1, 0),
            dw_kv[:, :HEAD_DIM],
            dw_kv[:, HEAD_DIM:],
            dot(grads, attended, 1, 0),
        ]
    ).astype(bf16)
    total = pick(dw, x).astype(f32)
    for s in (1, 2, 3):
        got = shift(pick(dw, (x - s) % 4), "x", 4, 1, s)
        total = total + got.astype(f32)
    send = jnp.concatenate([part, d_tokens], 1).reshape(8, 128, 512)
    got = a2a(send, "y").reshape(4, 2, 128, 512)
    back = jnp.sum(got.astype(f32), 0)
    back = back.reshape(2, 2, 2, WIDTH, 4, 128).transpose(2, 1, 0, 4, 3, 5)
    far = swap(back[1].astype(bf16), "zh")
    back = back[0] + far.astype(f32)
    other = swap(back[1], "c")
    back = jnp.stack(in_order(back[0], other, c))
    attention = join_tiles(back[:, :, :2].astype(bf16))
    token_grads = join_tiles(back[:, :, 2:])

    total = total.reshape(8, 2, 64, 128)
    got = swap(total[:, 1].astype(bf16), "c")
    total = (total[:, 0] + got.astype(f32)).astype(bf16).reshape(8, 2, WIDTH, 128)
    got = swap(total[:, 1], "zh")
    total = jnp.stack(in_order(total[:, 0], got, zh), 1)
    total = a2a(total, "y")
    total = jnp.sum(total.reshape(4, 2, 2, WIDTH, 128).astype(f32), 1).astype(bf16)
    total = total.transpose(1, 0, 2, 3).reshape(1, HEADS, WIDTH, 128)
    total = jnp.broadcast_to(total, (6, HEADS, WIDTH, 128))
    total = a2a(total, "zl")
    total = jnp.sum(total.astype(f32), 0).astype(bf16)
    got = swap(total, "x")
    total = jnp.stack(in_order(total, got, x % 2))
    got = lax.ppermute(total, "x", SWAP_X2)
    total = jnp.concatenate(in_order(total, got, x // 2))
    weight_grads = total.transpose(2, 0, 1, 3).astype(f32)
    return attention, token_grads, weight_grads


def solution(mesh):
    inner = Mesh(mesh.devices.reshape(SIZES), AXES)
    strips = P(("zl", "x"), ("zh", "y", "c"), None, None)
    rows = P(("zh", "y", "c"), None, None, None)
    return jax.shard_map(
        work,
        mesh=inner,
        in_specs=(strips, strips, rows),
        out_specs=(strips, strips, rows),
        check_vma=False,
    )
```

```python
import jax
import jax.numpy as jnp
from jax import lax
from jax.sharding import Mesh, PartitionSpec as P


D = 1024
HEADS = 8
HEAD_DIM = 128
TILE_ROWS = 16
TILE_COLS = 16
RIM = 4
PAD_ROWS = 24
PAD_COLS = 24
TILE_TOKENS = 256
PAD_TOKENS = 576
WIDTH = 32
ROWS_TOTAL = 192
COLS_TOTAL = 128

AXES = ("zl", "x", "zh", "y", "c")
SIZES = (6, 4, 2, 8, 2)

bf16 = jnp.bfloat16
f32 = jnp.float32


def right_pairs():
    pairs = []
    for x in range(4):
        for y in range(8):
            for c in range(2):
                col = (x % 2) * 4 + (y % 2) * 2 + c + 1
                if col < 8:
                    k = col % 4
                    to = (x - x % 2 + col // 4, y - y % 2 + k // 2, k % 2)
                    pairs.append((x * 16 + y * 2 + c, to[0] * 16 + to[1] * 2 + to[2]))
    return pairs


RIGHT = right_pairs()
LEFT = [(b, a) for a, b in RIGHT]
DOWN = [(t, t + 2) for t in range(22)]
UP = [(t + 2, t) for t in range(22)]
SWAP_X2 = [(i, i ^ 2) for i in range(4)]


def to_right(v):
    return lax.ppermute(v, ("x", "y", "c"), RIGHT)


def to_left(v):
    return lax.ppermute(v, ("x", "y", "c"), LEFT)


def to_down(v):
    return lax.ppermute(v, ("zl", "x"), DOWN)


def to_up(v):
    return lax.ppermute(v, ("zl", "x"), UP)


def a2a(v, axes):
    return lax.all_to_all(v, axes, 0, 0, tiled=True)


def dot(a, b, da, db):
    return lax.dot_general(a, b, (((da,), (db,)), ((), ())), preferred_element_type=f32)


def shift(v, axis, count, step, by):
    size = lax.axis_size(axis)
    ring = count * step
    pairs = []
    for i in range(size):
        base = i - i % ring
        pairs.append((i, base + (i % ring - by * step) % ring))
    return lax.ppermute(v, axis, pairs)


def swap(v, axis):
    return lax.ppermute(v, axis, [(i, i ^ 1) for i in range(lax.axis_size(axis))])


def pick(v, index, axis=0):
    return lax.dynamic_index_in_dim(v, index, axis, keepdims=False)


def in_order(mine, other, bit):
    first = bit == 0
    return jnp.where(first, mine, other), jnp.where(first, other, mine)


def split_tiles(block):
    return (
        block.reshape(WIDTH, 2, 8, 2, 2, TILE_COLS)
        .transpose(3, 4, 1, 0, 2, 5)
        .reshape(2, 2, 2, WIDTH, 128)
    )


def join_tiles(tiles):
    return (
        tiles.reshape(2, 2, 2, WIDTH, 8, TILE_COLS)
        .transpose(3, 2, 4, 1, 0, 5)
        .reshape(1, WIDTH, TILE_ROWS, 64)
    )


def work(embedded, cotangent, weights):
    score_scale = HEAD_DIM ** (-0.5)
    zl = lax.axis_index("zl")
    x = lax.axis_index("x")
    zh = lax.axis_index("zh")
    y = lax.axis_index("y")
    c = lax.axis_index("c")

    w_mine = pick(weights, x, 1).transpose(1, 0, 2)
    w_keep = lax.dynamic_slice_in_dim(w_mine, zh * 4, 4, 0)
    w_give = lax.dynamic_slice_in_dim(w_mine, (1 - zh) * 4, 4, 0)
    tiles = jnp.concatenate([split_tiles(embedded[0]), split_tiles(cotangent[0])], 2)
    mine = jnp.concatenate([tiles.reshape(16, WIDTH, 128), w_give])
    got = swap(mine, "zh")
    pairs = jnp.stack([tiles, got[:16].reshape(2, 2, 4, WIDTH, 128)], 3)
    t_keep = pick(pairs, c, 1)
    t_give = pick(pairs, 1 - c, 1)
    w_keep = jnp.stack([w_keep, got[16:]], 1)
    got = swap(t_give, "c")
    t_mine = jnp.stack([t_keep, got], 2)
    t_mine = t_mine.reshape(2, 4, 128, 128)
    t_mine = t_mine.transpose(0, 2, 1, 3)

    w_send = jnp.broadcast_to(w_keep.reshape(4, 1, 64, HEAD_DIM), (4, 2, 64, HEAD_DIM))
    w_x = a2a(w_send.reshape(8, 64, HEAD_DIM), "y")
    send = jnp.broadcast_to(t_mine.reshape(1, 2, 128, 512), (4, 2, 128, 512))
    both = a2a(send.reshape(8, 128, 512), "y").reshape(D, 512)
    tokens, grads = both[:, :TILE_TOKENS], both[:, TILE_TOKENS:]
    w_list = jnp.stack([w_x] + [shift(w_x, "x", 4, 1, s) for s in (1, 2, 3)])
    got = swap(w_list, "c")
    w_list = jnp.stack([w_list, got], 2).reshape(4, D, HEAD_DIM)
    w_qkv = jnp.concatenate([pick(w_list, (m - x) % 4) for m in range(3)], 1)
    w_out = pick(w_list, (3 - x) % 4)

    qkv = dot(tokens, w_qkv, 0, 0).astype(bf16)
    queries = qkv[:, :HEAD_DIM]
    kv = qkv[:, HEAD_DIM:].reshape(TILE_ROWS, TILE_COLS, 2 * HEAD_DIM)
    from_left = to_right(kv[:, TILE_COLS - RIM :])
    from_right = to_left(kv[:, :RIM])
    wide = jnp.concatenate([from_left, kv, from_right], 1)
    from_above = to_down(wide[TILE_ROWS - RIM :])
    from_below = to_up(wide[:RIM])
    window = jnp.concatenate([from_above, wide, from_below], 0).reshape(PAD_TOKENS, 2 * HEAD_DIM)
    keys = window[:, :HEAD_DIM]
    values = window[:, HEAD_DIM:]

    row_pos = (zl * 2 + x // 2) * TILE_ROWS + jnp.arange(PAD_ROWS) - RIM
    col_pos = ((x % 2) * 4 + (y % 2) * 2 + c) * TILE_COLS + jnp.arange(PAD_COLS) - RIM
    key_valid = (
        ((row_pos >= 0) & (row_pos < ROWS_TOTAL))[:, None]
        & ((col_pos >= 0) & (col_pos < COLS_TOTAL))[None, :]
    ).reshape(PAD_TOKENS)

    scores = dot(queries, keys, 1, 1) * score_scale
    scores = jnp.where(key_valid[None, :], scores, -jnp.inf)
    top_score = jnp.max(scores, axis=-1, keepdims=True)
    expo = jnp.exp(scores - top_score)
    probs = expo / jnp.sum(expo, axis=-1, keepdims=True)
    probs_low = probs.astype(bf16)
    attended = dot(probs_low, values, 1, 0).astype(bf16)
    part = dot(w_out, attended, 1, 1).astype(bf16)
    d_attended = dot(grads, w_out, 0, 0).astype(bf16)
    d_probs = dot(d_attended, values, 1, 1)
    d_scores = (
        probs * (d_probs - jnp.sum(d_probs * probs, axis=-1, keepdims=True)) * score_scale
    ).astype(bf16)
    d_queries = dot(d_scores, keys, 1, 0).astype(bf16)
    d_keys = dot(d_scores, queries, 0, 0)
    d_values = dot(probs_low, d_attended, 0, 0)
    d_window = jnp.concatenate([d_keys, d_values], 1).astype(bf16)
    d_window = d_window.reshape(PAD_ROWS, PAD_COLS, 2 * HEAD_DIM)
    back_below = to_up(d_window[:RIM])
    back_above = to_down(d_window[RIM + TILE_ROWS :])
    d_mid = d_window[RIM : RIM + TILE_ROWS].astype(f32)
    d_mid = (
        d_mid
        + jnp.pad(back_below.astype(f32), ((TILE_ROWS - RIM, 0), (0, 0), (0, 0)))
        + jnp.pad(back_above.astype(f32), ((0, TILE_ROWS - RIM), (0, 0), (0, 0)))
    )
    back_right = to_left(d_mid[:, :RIM].astype(bf16))
    back_left = to_right(d_mid[:, RIM + TILE_COLS :].astype(bf16))
    d_kv = (
        d_mid[:, RIM : RIM + TILE_COLS]
        + jnp.pad(back_right.astype(f32), ((0, 0), (TILE_COLS - RIM, 0), (0, 0)))
        + jnp.pad(back_left.astype(f32), ((0, 0), (0, TILE_COLS - RIM), (0, 0)))
    )
    d_kv = d_kv.astype(bf16).reshape(TILE_TOKENS, 2 * HEAD_DIM)
    d_qkv = jnp.concatenate([d_queries, d_kv], 1)

    d_tokens = dot(w_qkv, d_qkv, 1, 1).astype(bf16)
    dw_kv = dot(tokens, d_kv, 1, 0)
    dw = jnp.stack(
        [
            dot(tokens, d_queries, 1, 0),
            dw_kv[:, :HEAD_DIM],
            dw_kv[:, HEAD_DIM:],
            dot(grads, attended, 1, 0),
        ]
    ).astype(bf16)
    dw = dw.reshape(4, 8, 2, 64, HEAD_DIM)
    got = swap(dw[:, :, 1], "c")
    dw = (dw[:, :, 0].astype(f32) + got.astype(f32)).astype(bf16)
    total = pick(dw, x).astype(f32)
    for s in (1, 2, 3):
        got = shift(pick(dw, (x - s) % 4), "x", 4, 1, s)
        total = total + got.astype(f32)
    send = jnp.concatenate([part, d_tokens], 1).reshape(8, 128, 512)
    got = a2a(send, "y").reshape(4, 2, 128, 512)
    back = jnp.sum(got.astype(f32), 0)
    back = back.reshape(2, 2, 2, WIDTH, 4, 128).transpose(2, 1, 0, 4, 3, 5)
    far = swap(back[1].astype(bf16), "zh")
    back = back[0] + far.astype(f32)
    other = swap(back[1], "c")
    back = jnp.stack(in_order(back[0], other, c))
    attention = join_tiles(back[:, :, :2].astype(bf16))
    token_grads = join_tiles(back[:, :, 2:])

    total = a2a(total.astype(bf16), "y")
    total = jnp.sum(total.reshape(4, 2, 2, WIDTH, 128).astype(f32), 1).astype(bf16)
    total = jnp.stack(in_order(total[:, 0], total[:, 1], zh))
    total = jnp.broadcast_to(total, (6, 2, 4, WIDTH, 128)).reshape(12, 4, WIDTH, 128)
    total = a2a(total, ("zl", "zh"))
    total = jnp.sum(total.reshape(6, HEADS, WIDTH, 128).astype(f32), 0).astype(bf16)
    got = swap(total, "x")
    total = jnp.stack(in_order(total, got, x % 2))
    got = lax.ppermute(total, "x", SWAP_X2)
    total = jnp.concatenate(in_order(total, got, x // 2))
    weight_grads = total.transpose(2, 0, 1, 3).astype(f32)
    return attention, token_grads, weight_grads


def solution(mesh):
    inner = Mesh(mesh.devices.reshape(SIZES), AXES)
    strips = P(("zl", "x"), ("zh", "y", "c"), None, None)
    rows = P(("zh", "y", "c"), None, None, None)
    return jax.shard_map(
        work,
        mesh=inner,
        in_specs=(strips, strips, rows),
        out_specs=(strips, strips, rows),
        check_vma=False,
    )
```

```python
import jax
import jax.numpy as jnp
from jax import lax
from jax.sharding import Mesh, PartitionSpec as P


D = 1024
HEADS = 8
HEAD_DIM = 128
TILE_ROWS = 16
TILE_COLS = 16
RIM = 4
PAD_ROWS = 24
PAD_COLS = 24
TILE_TOKENS = 256
PAD_TOKENS = 576
WIDTH = 32
ROWS_TOTAL = 192
COLS_TOTAL = 128

AXES = ("zl", "x", "zh", "y", "c")
SIZES = (6, 4, 2, 8, 2)

bf16 = jnp.bfloat16
f32 = jnp.float32


def right_pairs():
    pairs = []
    for x in range(4):
        for y in range(8):
            for c in range(2):
                col = (x % 2) * 4 + (y % 2) * 2 + c + 1
                if col < 8:
                    k = col % 4
                    to = (x - x % 2 + col // 4, y - y % 2 + k // 2, k % 2)
                    pairs.append((x * 16 + y * 2 + c, to[0] * 16 + to[1] * 2 + to[2]))
    return pairs


RIGHT = right_pairs()
LEFT = [(b, a) for a, b in RIGHT]
DOWN = [(t, t + 2) for t in range(22)]
UP = [(t + 2, t) for t in range(22)]


def to_right(v):
    return lax.ppermute(v, ("x", "y", "c"), RIGHT)


def to_left(v):
    return lax.ppermute(v, ("x", "y", "c"), LEFT)


def to_down(v):
    return lax.ppermute(v, ("zl", "x"), DOWN)


def to_up(v):
    return lax.ppermute(v, ("zl", "x"), UP)


def a2a(v, axes):
    return lax.all_to_all(v, axes, 0, 0, tiled=True)


def dot(a, b, da, db):
    return lax.dot_general(a, b, (((da,), (db,)), ((), ())), preferred_element_type=f32)


def shift(v, axis, count, step, by):
    size = lax.axis_size(axis)
    ring = count * step
    pairs = []
    for i in range(size):
        base = i - i % ring
        pairs.append((i, base + (i % ring - by * step) % ring))
    return lax.ppermute(v, axis, pairs)


def swap(v, axis):
    return lax.ppermute(v, axis, [(i, i ^ 1) for i in range(lax.axis_size(axis))])


def pick(v, index, axis=0):
    return lax.dynamic_index_in_dim(v, index, axis, keepdims=False)


def in_order(mine, other, bit):
    first = bit == 0
    return jnp.where(first, mine, other), jnp.where(first, other, mine)


def split_tiles(block):
    return (
        block.reshape(WIDTH, 2, 8, 2, 2, TILE_COLS)
        .transpose(3, 4, 1, 0, 2, 5)
        .reshape(2, 2, 2, WIDTH, 128)
    )


def join_tiles(tiles):
    return (
        tiles.reshape(2, 2, 2, WIDTH, 8, TILE_COLS)
        .transpose(3, 2, 4, 1, 0, 5)
        .reshape(1, WIDTH, TILE_ROWS, 64)
    )


def work(embedded, cotangent, weights):
    score_scale = HEAD_DIM ** (-0.5)
    zl = lax.axis_index("zl")
    x = lax.axis_index("x")
    zh = lax.axis_index("zh")
    y = lax.axis_index("y")
    c = lax.axis_index("c")

    w_mine = pick(weights, x, 1).transpose(1, 0, 2)
    w_keep = lax.dynamic_slice_in_dim(w_mine, zh * 4, 4, 0)
    w_give = lax.dynamic_slice_in_dim(w_mine, (1 - zh) * 4, 4, 0)
    tiles = jnp.concatenate([split_tiles(embedded[0]), split_tiles(cotangent[0])], 2)
    mine = jnp.concatenate([tiles.reshape(16, WIDTH, 128), w_give])
    got = swap(mine, "zh")
    pairs = jnp.stack([tiles, got[:16].reshape(2, 2, 4, WIDTH, 128)], 3)
    t_keep = pick(pairs, c, 1)
    t_give = pick(pairs, 1 - c, 1)
    w_keep = jnp.stack([w_keep, got[16:]], 1)
    got = swap(t_give, "c")
    t_mine = jnp.stack([t_keep, got], 2)
    t_mine = t_mine.reshape(2, 4, 128, 128)
    t_mine = t_mine.transpose(0, 2, 1, 3)

    w_send = jnp.broadcast_to(w_keep.reshape(4, 1, 64, HEAD_DIM), (4, 2, 64, HEAD_DIM))
    w_x = a2a(w_send.reshape(8, 64, HEAD_DIM), "y")

    def gather(v):
        send = jnp.broadcast_to(v.reshape(1, 2, 128, TILE_TOKENS), (4, 2, 128, TILE_TOKENS))
        return a2a(send.reshape(8, 128, TILE_TOKENS), "y").reshape(D, TILE_TOKENS)

    tokens = gather(t_mine[:, :, :2])
    grads = gather(t_mine[:, :, 2:])
    w_list = jnp.stack([w_x] + [shift(w_x, "x", 4, 1, s) for s in (1, 2, 3)])
    got = swap(w_list, "c")
    w_list = jnp.stack([w_list, got], 2).reshape(4, D, HEAD_DIM)
    w_qkv = jnp.concatenate([pick(w_list, (m - x) % 4) for m in range(3)], 1)
    w_out = pick(w_list, (3 - x) % 4)

    qkv = dot(tokens, w_qkv, 0, 0).astype(bf16)
    queries = qkv[:, :HEAD_DIM]
    kv = qkv[:, HEAD_DIM:].reshape(TILE_ROWS, TILE_COLS, 2 * HEAD_DIM)
    from_left = to_right(kv[:, TILE_COLS - RIM :])
    from_right = to_left(kv[:, :RIM])
    wide = jnp.concatenate([from_left, kv, from_right], 1)
    from_above = to_down(wide[TILE_ROWS - RIM :])
    from_below = to_up(wide[:RIM])
    window = jnp.concatenate([from_above, wide, from_below], 0).reshape(PAD_TOKENS, 2 * HEAD_DIM)
    keys = window[:, :HEAD_DIM]
    values = window[:, HEAD_DIM:]

    row_pos = (zl * 2 + x // 2) * TILE_ROWS + jnp.arange(PAD_ROWS) - RIM
    col_pos = ((x % 2) * 4 + (y % 2) * 2 + c) * TILE_COLS + jnp.arange(PAD_COLS) - RIM
    key_valid = (
        ((row_pos >= 0) & (row_pos < ROWS_TOTAL))[:, None]
        & ((col_pos >= 0) & (col_pos < COLS_TOTAL))[None, :]
    ).reshape(PAD_TOKENS)

    scores = dot(queries, keys, 1, 1) * score_scale
    scores = jnp.where(key_valid[None, :], scores, -jnp.inf)
    top_score = jnp.max(scores, axis=-1, keepdims=True)
    expo = jnp.exp(scores - top_score)
    probs = expo / jnp.sum(expo, axis=-1, keepdims=True)
    probs_low = probs.astype(bf16)
    attended = dot(probs_low, values, 1, 0).astype(bf16)
    part = dot(w_out, attended, 1, 1).astype(bf16)
    d_attended = dot(grads, w_out, 0, 0).astype(bf16)
    d_probs = dot(d_attended, values, 1, 1)
    d_scores = (
        probs * (d_probs - jnp.sum(d_probs * probs, axis=-1, keepdims=True)) * score_scale
    ).astype(bf16)
    d_queries = dot(d_scores, keys, 1, 0).astype(bf16)
    d_keys = dot(d_scores, queries, 0, 0)
    d_values = dot(probs_low, d_attended, 0, 0)
    d_window = jnp.concatenate([d_keys, d_values], 1).astype(bf16)
    d_window = d_window.reshape(PAD_ROWS, PAD_COLS, 2 * HEAD_DIM)
    back_below = to_up(d_window[:RIM])
    back_above = to_down(d_window[RIM + TILE_ROWS :])
    d_mid = d_window[RIM : RIM + TILE_ROWS].astype(f32)
    d_mid = (
        d_mid
        + jnp.pad(back_below.astype(f32), ((TILE_ROWS - RIM, 0), (0, 0), (0, 0)))
        + jnp.pad(back_above.astype(f32), ((0, TILE_ROWS - RIM), (0, 0), (0, 0)))
    )
    back_right = to_left(d_mid[:, :RIM].astype(bf16))
    back_left = to_right(d_mid[:, RIM + TILE_COLS :].astype(bf16))
    d_kv = (
        d_mid[:, RIM : RIM + TILE_COLS]
        + jnp.pad(back_right.astype(f32), ((0, 0), (TILE_COLS - RIM, 0), (0, 0)))
        + jnp.pad(back_left.astype(f32), ((0, 0), (0, TILE_COLS - RIM), (0, 0)))
    )
    d_kv = d_kv.astype(bf16).reshape(TILE_TOKENS, 2 * HEAD_DIM)
    d_qkv = jnp.concatenate([d_queries, d_kv], 1)

    d_tokens = dot(w_qkv, d_qkv, 1, 1).astype(bf16)
    dw_kv = dot(tokens, d_kv, 1, 0)
    dw = jnp.stack(
        [
            dot(tokens, d_queries, 1, 0),
            dw_kv[:, :HEAD_DIM],
            dw_kv[:, HEAD_DIM:],
            dot(grads, attended, 1, 0),
        ]
    ).astype(bf16)
    dw = dw.reshape(4, 8, 2, 64, HEAD_DIM)
    got = swap(dw[:, :, 1], "c")
    dw = (dw[:, :, 0].astype(f32) + got.astype(f32)).astype(bf16)
    total = pick(dw, x).astype(f32)
    for s in (1, 2, 3):
        got = shift(pick(dw, (x - s) % 4), "x", 4, 1, s)
        total = total + got.astype(f32)
    send = jnp.concatenate([part, d_tokens], 1).reshape(8, 128, 512)
    got = a2a(send, "y").reshape(4, 2, 128, 512)
    back = jnp.sum(got.astype(f32), 0)
    back = back.reshape(2, 2, 2, WIDTH, 4, 128).transpose(2, 1, 0, 4, 3, 5)
    far = swap(back[1].astype(bf16), "zh")
    back = back[0] + far.astype(f32)
    other = swap(back[1], "c")
    back = jnp.stack(in_order(back[0], other, c))
    attention = join_tiles(back[:, :, :2].astype(bf16))
    token_grads = join_tiles(back[:, :, 2:])

    total = a2a(total.astype(bf16), "y")
    total = jnp.sum(total.reshape(4, 2, 2, WIDTH, 128).astype(f32), 1).astype(bf16)
    total = jnp.stack(in_order(total[:, 0], total[:, 1], zh))
    total = jnp.pad(total.reshape(2, 128, 128), ((0, 0), (0, 16), (0, 0)))
    total = total.reshape(2, 6, 24, 128).transpose(1, 0, 2, 3).reshape(12, 24, 128)
    total = a2a(total, ("zl", "zh"))
    total = jnp.sum(total.reshape(6, 1, 48, 128).astype(f32), 0).astype(bf16)
    total = jnp.broadcast_to(total, (24, 48, 128))
    total = a2a(total, ("zl", "x"))
    total = total.reshape(6, 4, 2, 24, 128).transpose(1, 2, 0, 3, 4).reshape(4, 2, 144, 128)
    total = total[:, :, :128].reshape(4, HEADS, WIDTH, 128)
    weight_grads = total.transpose(2, 0, 1, 3).astype(f32)
    return attention, token_grads, weight_grads


def solution(mesh):
    inner = Mesh(mesh.devices.reshape(SIZES), AXES)
    strips = P(("zl", "x"), ("zh", "y", "c"), None, None)
    rows = P(("zh", "y", "c"), None, None, None)
    return jax.shard_map(
        work,
        mesh=inner,
        in_specs=(strips, strips, rows),
        out_specs=(strips, strips, rows),
        check_vma=False,
    )
```

```python
import jax
import jax.numpy as jnp
from jax import lax
from jax.sharding import Mesh, PartitionSpec as P


D = 1024
HEADS = 8
HEAD_DIM = 128
TILE_ROWS = 16
TILE_COLS = 16
RIM = 4
PAD_ROWS = 24
PAD_COLS = 24
TILE_TOKENS = 256
PAD_TOKENS = 576
WIDTH = 32
ROWS_TOTAL = 192
COLS_TOTAL = 128

AXES = ("zl", "x", "zh", "y", "c")
SIZES = (6, 4, 2, 8, 2)

bf16 = jnp.bfloat16
f32 = jnp.float32


def right_pairs():
    pairs = []
    for x in range(4):
        for y in range(8):
            for c in range(2):
                col = (x % 2) * 4 + (y % 2) * 2 + c + 1
                if col < 8:
                    k = col % 4
                    to = (x - x % 2 + col // 4, y - y % 2 + k // 2, k % 2)
                    pairs.append((x * 16 + y * 2 + c, to[0] * 16 + to[1] * 2 + to[2]))
    return pairs


RIGHT = right_pairs()
LEFT = [(b, a) for a, b in RIGHT]
DOWN = [(t, t + 2) for t in range(22)]
UP = [(t + 2, t) for t in range(22)]


def to_right(v):
    return lax.ppermute(v, ("x", "y", "c"), RIGHT)


def to_left(v):
    return lax.ppermute(v, ("x", "y", "c"), LEFT)


def to_down(v):
    return lax.ppermute(v, ("zl", "x"), DOWN)


def to_up(v):
    return lax.ppermute(v, ("zl", "x"), UP)


def a2a(v, axes):
    return lax.all_to_all(v, axes, 0, 0, tiled=True)


def dot(a, b, da, db):
    return lax.dot_general(a, b, (((da,), (db,)), ((), ())), preferred_element_type=f32)


def shift(v, axis, count, step, by):
    size = lax.axis_size(axis)
    ring = count * step
    pairs = []
    for i in range(size):
        base = i - i % ring
        pairs.append((i, base + (i % ring - by * step) % ring))
    return lax.ppermute(v, axis, pairs)


def swap(v, axis):
    return lax.ppermute(v, axis, [(i, i ^ 1) for i in range(lax.axis_size(axis))])


def pick(v, index, axis=0):
    return lax.dynamic_index_in_dim(v, index, axis, keepdims=False)


def in_order(mine, other, bit):
    first = bit == 0
    return jnp.where(first, mine, other), jnp.where(first, other, mine)


def split_tiles(block):
    return (
        block.reshape(WIDTH, 2, 8, 2, 2, TILE_COLS)
        .transpose(3, 4, 1, 0, 2, 5)
        .reshape(2, 2, 2, WIDTH, 128)
    )


def join_tiles(tiles):
    return (
        tiles.reshape(2, 2, 2, WIDTH, 8, TILE_COLS)
        .transpose(3, 2, 4, 1, 0, 5)
        .reshape(1, WIDTH, TILE_ROWS, 64)
    )


def work(embedded, cotangent, weights):
    score_scale = HEAD_DIM ** (-0.5)
    zl = lax.axis_index("zl")
    x = lax.axis_index("x")
    zh = lax.axis_index("zh")
    y = lax.axis_index("y")
    c = lax.axis_index("c")

    w_mine = pick(weights, x, 1).transpose(1, 0, 2)
    w_keep = lax.dynamic_slice_in_dim(w_mine, zh * 4, 4, 0)
    w_give = lax.dynamic_slice_in_dim(w_mine, (1 - zh) * 4, 4, 0)
    tiles = jnp.concatenate([split_tiles(embedded[0]), split_tiles(cotangent[0])], 2)
    mine = jnp.concatenate([tiles.reshape(16, WIDTH, 128), w_give])
    got = swap(mine, "zh")
    pairs = jnp.stack([tiles, got[:16].reshape(2, 2, 4, WIDTH, 128)], 3)
    t_keep = pick(pairs, c, 1)
    t_give = pick(pairs, 1 - c, 1)
    w_keep = jnp.stack([w_keep, got[16:]], 1)
    got = swap(t_give, "c")
    t_mine = jnp.stack([t_keep, got], 2)
    t_mine = t_mine.reshape(2, 4, 128, 128)
    t_mine = t_mine.transpose(0, 2, 1, 3)

    w_send = jnp.broadcast_to(w_keep.reshape(4, 1, 64, HEAD_DIM), (4, 2, 64, HEAD_DIM))
    w_x = a2a(w_send.reshape(8, 64, HEAD_DIM), "y")
    send = jnp.broadcast_to(t_mine.reshape(1, 2, 128, 512), (4, 2, 128, 512))
    both = a2a(send.reshape(8, 128, 512), "y").reshape(D, 512)
    tokens, grads = both[:, :TILE_TOKENS], both[:, TILE_TOKENS:]
    w_list = jnp.stack([w_x] + [shift(w_x, "x", 4, 1, s) for s in (1, 2, 3)])
    got = swap(w_list, "c")
    w_list = jnp.stack([w_list, got], 2).reshape(4, D, HEAD_DIM)
    w_qkv = jnp.concatenate([pick(w_list, (m - x) % 4) for m in range(3)], 1)
    w_out = pick(w_list, (3 - x) % 4)

    qkv = dot(tokens, w_qkv, 0, 0).astype(bf16)
    queries = qkv[:, :HEAD_DIM]
    kv = qkv[:, HEAD_DIM:].reshape(TILE_ROWS, TILE_COLS, 2 * HEAD_DIM)
    from_left = to_right(kv[:, TILE_COLS - RIM :])
    from_right = to_left(kv[:, :RIM])
    wide = jnp.concatenate([from_left, kv, from_right], 1)
    from_above = to_down(wide[TILE_ROWS - RIM :])
    from_below = to_up(wide[:RIM])
    window = jnp.concatenate([from_above, wide, from_below], 0).reshape(PAD_TOKENS, 2 * HEAD_DIM)
    keys = window[:, :HEAD_DIM]
    values = window[:, HEAD_DIM:]

    row_pos = (zl * 2 + x // 2) * TILE_ROWS + jnp.arange(PAD_ROWS) - RIM
    col_pos = ((x % 2) * 4 + (y % 2) * 2 + c) * TILE_COLS + jnp.arange(PAD_COLS) - RIM
    key_valid = (
        ((row_pos >= 0) & (row_pos < ROWS_TOTAL))[:, None]
        & ((col_pos >= 0) & (col_pos < COLS_TOTAL))[None, :]
    ).reshape(PAD_TOKENS)

    scores = dot(queries, keys, 1, 1) * score_scale
    scores = jnp.where(key_valid[None, :], scores, -jnp.inf)
    top_score = jnp.max(scores, axis=-1, keepdims=True)
    expo = jnp.exp(scores - top_score)
    probs = expo / jnp.sum(expo, axis=-1, keepdims=True)
    probs_low = probs.astype(bf16)
    attended = dot(probs_low, values, 1, 0).astype(bf16)
    part = dot(w_out, attended, 1, 1).astype(bf16)
    d_attended = dot(grads, w_out, 0, 0).astype(bf16)
    d_probs = dot(d_attended, values, 1, 1)
    d_scores = (
        probs * (d_probs - jnp.sum(d_probs * probs, axis=-1, keepdims=True)) * score_scale
    ).astype(bf16)
    d_queries = dot(d_scores, keys, 1, 0).astype(bf16)
    d_keys = dot(d_scores, queries, 0, 0)
    d_values = dot(probs_low, d_attended, 0, 0)
    d_window = jnp.concatenate([d_keys, d_values], 1).astype(bf16)
    d_window = d_window.reshape(PAD_ROWS, PAD_COLS, 2 * HEAD_DIM)
    back_below = to_up(d_window[:RIM])
    back_above = to_down(d_window[RIM + TILE_ROWS :])
    d_mid = d_window[RIM : RIM + TILE_ROWS].astype(f32)
    d_mid = (
        d_mid
        + jnp.pad(back_below.astype(f32), ((TILE_ROWS - RIM, 0), (0, 0), (0, 0)))
        + jnp.pad(back_above.astype(f32), ((0, TILE_ROWS - RIM), (0, 0), (0, 0)))
    )
    back_right = to_left(d_mid[:, :RIM].astype(bf16))
    back_left = to_right(d_mid[:, RIM + TILE_COLS :].astype(bf16))
    d_kv = (
        d_mid[:, RIM : RIM + TILE_COLS]
        + jnp.pad(back_right.astype(f32), ((0, 0), (TILE_COLS - RIM, 0), (0, 0)))
        + jnp.pad(back_left.astype(f32), ((0, 0), (0, TILE_COLS - RIM), (0, 0)))
    )
    d_kv = d_kv.astype(bf16).reshape(TILE_TOKENS, 2 * HEAD_DIM)
    d_qkv = jnp.concatenate([d_queries, d_kv], 1)

    d_tokens = dot(w_qkv, d_qkv, 1, 1).astype(bf16)
    dw_kv = dot(tokens, d_kv, 1, 0)
    dw = jnp.stack(
        [
            dot(tokens, d_queries, 1, 0),
            dw_kv[:, :HEAD_DIM],
            dw_kv[:, HEAD_DIM:],
            dot(grads, attended, 1, 0),
        ]
    ).astype(bf16)
    dw = dw.reshape(4, 8, 2, 64, HEAD_DIM)
    got = swap(dw[:, :, 1], "c")
    dw = (dw[:, :, 0].astype(f32) + got.astype(f32)).astype(bf16)
    total = pick(dw, x).astype(f32)
    for s in (1, 2, 3):
        got = shift(pick(dw, (x - s) % 4), "x", 4, 1, s)
        total = total + got.astype(f32)
    send = jnp.concatenate([part, d_tokens], 1).reshape(8, 128, 512)
    got = a2a(send, "y").reshape(4, 2, 128, 512)
    back = jnp.sum(got.astype(f32), 0)
    back = back.reshape(2, 2, 2, WIDTH, 4, 128).transpose(2, 1, 0, 4, 3, 5)
    far = swap(back[1].astype(bf16), "zh")
    back = back[0] + far.astype(f32)
    other = swap(back[1], "c")
    back = jnp.stack(in_order(back[0], other, c))
    attention = join_tiles(back[:, :, :2].astype(bf16))
    token_grads = join_tiles(back[:, :, 2:])

    total = a2a(total.astype(bf16), "y")
    total = jnp.sum(total.reshape(4, 2, 2, WIDTH, 128).astype(f32), 1).astype(bf16)
    total = jnp.stack(in_order(total[:, 0], total[:, 1], zh))
    total = jnp.pad(total.reshape(2, 128, 128), ((0, 0), (0, 16), (0, 0)))
    total = total.reshape(2, 6, 24, 128).transpose(1, 0, 2, 3).reshape(12, 24, 128)
    total = a2a(total, ("zl", "zh"))
    total = jnp.sum(total.reshape(6, 1, 48, 128).astype(f32), 0).astype(bf16)
    total = jnp.broadcast_to(total, (24, 48, 128))
    total = a2a(total, ("zl", "x"))
    total = total.reshape(6, 4, 2, 24, 128).transpose(1, 2, 0, 3, 4).reshape(4, 2, 144, 128)
    total = total[:, :, :128].reshape(4, HEADS, WIDTH, 128)
    weight_grads = total.transpose(2, 0, 1, 3).astype(f32)
    return attention, token_grads, weight_grads


def solution(mesh):
    inner = Mesh(mesh.devices.reshape(SIZES), AXES)
    strips = P(("zl", "x"), ("zh", "y", "c"), None, None)
    rows = P(("zh", "y", "c"), None, None, None)
    return jax.shard_map(
        work,
        mesh=inner,
        in_specs=(strips, strips, rows),
        out_specs=(strips, strips, rows),
        check_vma=False,
    )
```

```python
import jax
import jax.numpy as jnp
from jax import lax
from jax.sharding import Mesh, PartitionSpec as P


D = 1024
HEADS = 8
HEAD_DIM = 128
TILE_ROWS = 16
TILE_COLS = 16
RIM = 4
PAD_ROWS = 24
PAD_COLS = 24
TILE_TOKENS = 256
PAD_TOKENS = 576
WIDTH = 32
ROWS_TOTAL = 192
COLS_TOTAL = 128

AXES = ("zl", "x", "zh", "y", "c")
SIZES = (6, 4, 2, 8, 2)

bf16 = jnp.bfloat16
f32 = jnp.float32


def right_pairs():
    pairs = []
    for x in range(4):
        for y in range(8):
            for c in range(2):
                col = (x % 2) * 4 + (y % 2) * 2 + c + 1
                if col < 8:
                    k = col % 4
                    to = (x - x % 2 + col // 4, y - y % 2 + k // 2, k % 2)
                    pairs.append((x * 16 + y * 2 + c, to[0] * 16 + to[1] * 2 + to[2]))
    return pairs


RIGHT = right_pairs()
LEFT = [(b, a) for a, b in RIGHT]
DOWN = [(t, t + 2) for t in range(22)]
UP = [(t + 2, t) for t in range(22)]


def to_right(v):
    return lax.ppermute(v, ("x", "y", "c"), RIGHT)


def to_left(v):
    return lax.ppermute(v, ("x", "y", "c"), LEFT)


def to_down(v):
    return lax.ppermute(v, ("zl", "x"), DOWN)


def to_up(v):
    return lax.ppermute(v, ("zl", "x"), UP)


def a2a(v, axes):
    return lax.all_to_all(v, axes, 0, 0, tiled=True)


def dot(a, b, da, db):
    return lax.dot_general(a, b, (((da,), (db,)), ((), ())), preferred_element_type=f32)


def shift(v, axis, count, step, by):
    size = lax.axis_size(axis)
    ring = count * step
    pairs = []
    for i in range(size):
        base = i - i % ring
        pairs.append((i, base + (i % ring - by * step) % ring))
    return lax.ppermute(v, axis, pairs)


def swap(v, axis):
    return lax.ppermute(v, axis, [(i, i ^ 1) for i in range(lax.axis_size(axis))])


def pick(v, index, axis=0):
    return lax.dynamic_index_in_dim(v, index, axis, keepdims=False)


def in_order(mine, other, bit):
    first = bit == 0
    return jnp.where(first, mine, other), jnp.where(first, other, mine)


def split_tiles(block):
    return (
        block.reshape(WIDTH, 2, 8, 2, 2, TILE_COLS)
        .transpose(3, 4, 1, 0, 2, 5)
        .reshape(2, 2, 2, WIDTH, 128)
    )


def join_tiles(tiles):
    return (
        tiles.reshape(2, 2, 2, WIDTH, 8, TILE_COLS)
        .transpose(3, 2, 4, 1, 0, 5)
        .reshape(1, WIDTH, TILE_ROWS, 64)
    )


def work(embedded, cotangent, weights):
    score_scale = HEAD_DIM ** (-0.5)
    zl = lax.axis_index("zl")
    x = lax.axis_index("x")
    zh = lax.axis_index("zh")
    y = lax.axis_index("y")
    c = lax.axis_index("c")

    w_mine = pick(weights, x, 1).transpose(1, 0, 2)
    w_keep = lax.dynamic_slice_in_dim(w_mine, zh * 4, 4, 0)
    w_give = lax.dynamic_slice_in_dim(w_mine, (1 - zh) * 4, 4, 0)
    tiles = jnp.concatenate([split_tiles(embedded[0]), split_tiles(cotangent[0])], 2)
    mine = jnp.concatenate([tiles.reshape(16, WIDTH, 128), w_give])
    got = swap(mine, "zh")
    pairs = jnp.stack([tiles, got[:16].reshape(2, 2, 4, WIDTH, 128)], 3)
    t_keep = pick(pairs, c, 1)
    t_give = pick(pairs, 1 - c, 1)
    w_keep = jnp.stack([w_keep, got[16:]], 1)
    got = swap(t_give, "c")
    t_mine = jnp.stack([t_keep, got], 2)
    t_mine = t_mine.reshape(2, 4, 128, 128)
    t_mine = t_mine.transpose(0, 2, 1, 3)

    w_send = jnp.broadcast_to(w_keep.reshape(4, 1, 64, HEAD_DIM), (4, 2, 64, HEAD_DIM))
    w_x = a2a(w_send.reshape(8, 64, HEAD_DIM), "y")
    send = jnp.broadcast_to(t_mine.reshape(1, 2, 128, 512), (4, 2, 128, 512))
    both = a2a(send.reshape(8, 128, 512), "y").reshape(D, 512)
    tokens, grads = both[:, :TILE_TOKENS], both[:, TILE_TOKENS:]
    w_list = jnp.stack([w_x] + [shift(w_x, "x", 4, 1, s) for s in (1, 2, 3)])
    got = swap(w_list, "c")
    w_list = jnp.stack([w_list, got], 2).reshape(4, D, HEAD_DIM)
    w_qkv = jnp.concatenate([pick(w_list, (m - x) % 4) for m in range(3)], 1)
    w_out = pick(w_list, (3 - x) % 4)

    qkv = dot(tokens, w_qkv, 0, 0).astype(bf16)
    queries = qkv[:, :HEAD_DIM]
    kv = qkv[:, HEAD_DIM:].reshape(TILE_ROWS, TILE_COLS, 2 * HEAD_DIM)
    from_left = to_right(kv[:, TILE_COLS - RIM :])
    from_right = to_left(kv[:, :RIM])
    wide = jnp.concatenate([from_left, kv, from_right], 1)
    from_above = to_down(wide[TILE_ROWS - RIM :])
    from_below = to_up(wide[:RIM])
    window = jnp.concatenate([from_above, wide, from_below], 0).reshape(PAD_TOKENS, 2 * HEAD_DIM)
    keys = window[:, :HEAD_DIM]
    values = window[:, HEAD_DIM:]

    row_pos = (zl * 2 + x // 2) * TILE_ROWS + jnp.arange(PAD_ROWS) - RIM
    col_pos = ((x % 2) * 4 + (y % 2) * 2 + c) * TILE_COLS + jnp.arange(PAD_COLS) - RIM
    key_valid = (
        ((row_pos >= 0) & (row_pos < ROWS_TOTAL))[:, None]
        & ((col_pos >= 0) & (col_pos < COLS_TOTAL))[None, :]
    ).reshape(PAD_TOKENS)

    scores = dot(queries, keys, 1, 1) * score_scale
    scores = jnp.where(key_valid[None, :], scores, -jnp.inf)
    top_score = jnp.max(scores, axis=-1, keepdims=True)
    expo = jnp.exp(scores - top_score)
    probs = expo / jnp.sum(expo, axis=-1, keepdims=True)
    probs_low = probs.astype(bf16)
    attended = dot(probs_low, values, 1, 0).astype(bf16)
    part = dot(w_out, attended, 1, 1).astype(bf16)
    d_attended = dot(grads, w_out, 0, 0).astype(bf16)
    d_probs = dot(d_attended, values, 1, 1)
    d_scores = (
        probs * (d_probs - jnp.sum(d_probs * probs, axis=-1, keepdims=True)) * score_scale
    ).astype(bf16)
    d_queries = dot(d_scores, keys, 1, 0).astype(bf16)
    d_keys = dot(d_scores, queries, 0, 0)
    d_values = dot(probs_low, d_attended, 0, 0)
    d_window = jnp.concatenate([d_keys, d_values], 1).astype(bf16)
    d_window = d_window.reshape(PAD_ROWS, PAD_COLS, 2 * HEAD_DIM)
    back_below = to_up(d_window[:RIM])
    back_above = to_down(d_window[RIM + TILE_ROWS :])
    d_mid = d_window[RIM : RIM + TILE_ROWS].astype(f32)
    d_mid = (
        d_mid
        + jnp.pad(back_below.astype(f32), ((TILE_ROWS - RIM, 0), (0, 0), (0, 0)))
        + jnp.pad(back_above.astype(f32), ((0, TILE_ROWS - RIM), (0, 0), (0, 0)))
    )
    back_right = to_left(d_mid[:, :RIM].astype(bf16))
    back_left = to_right(d_mid[:, RIM + TILE_COLS :].astype(bf16))
    d_kv = (
        d_mid[:, RIM : RIM + TILE_COLS]
        + jnp.pad(back_right.astype(f32), ((0, 0), (TILE_COLS - RIM, 0), (0, 0)))
        + jnp.pad(back_left.astype(f32), ((0, 0), (0, TILE_COLS - RIM), (0, 0)))
    )
    d_kv = d_kv.astype(bf16).reshape(TILE_TOKENS, 2 * HEAD_DIM)
    d_qkv = jnp.concatenate([d_queries, d_kv], 1)

    d_tokens = dot(w_qkv, d_qkv, 1, 1).astype(bf16)
    dw_kv = dot(tokens, d_kv, 1, 0)
    dw = jnp.stack(
        [
            dot(tokens, d_queries, 1, 0),
            dw_kv[:, :HEAD_DIM],
            dw_kv[:, HEAD_DIM:],
            dot(grads, attended, 1, 0),
        ]
    ).astype(bf16)
    dw = dw.reshape(4, 8, 2, 64, HEAD_DIM)
    got = swap(dw[:, :, 1], "c")
    dw = (dw[:, :, 0].astype(f32) + got.astype(f32)).astype(bf16)
    total = pick(dw, x).astype(f32)
    for s in (1, 2, 3):
        got = shift(pick(dw, (x - s) % 4), "x", 4, 1, s)
        total = total + got.astype(f32)
    send = jnp.concatenate([part, d_tokens], 1).reshape(8, 128, 512)
    got = a2a(send, "y").reshape(4, 2, 128, 512)
    back = jnp.sum(got.astype(f32), 0)
    back = back.reshape(2, 2, 2, WIDTH, 4, 128).transpose(2, 1, 0, 4, 3, 5)
    far = swap(back[1].astype(bf16), "zh")
    back = back[0] + far.astype(f32)
    other = swap(back[1], "c")
    back = jnp.stack(in_order(back[0], other, c))
    attention = join_tiles(back[:, :, :2].astype(bf16))
    token_grads = join_tiles(back[:, :, 2:])

    total = total.astype(bf16).reshape(8, 2, WIDTH, 128)
    total = jnp.stack(in_order(total[:, 0], total[:, 1], zh))
    total = jnp.pad(total, ((0, 0), (0, 0), (0, 16), (0, 0))).reshape(2, 8, 6, 8, 128)
    total = total.transpose(2, 0, 1, 3, 4).reshape(96, 8, 128)
    total = a2a(total, ("zl", "zh", "y"))
    total = jnp.sum(total.reshape(6, 8, 2, 8, 128).astype(f32), (0, 2))
    total = jnp.broadcast_to(total.astype(bf16).reshape(1, 64, 128), (24, 64, 128))
    total = a2a(total, ("zl", "x"))
    total = total.reshape(6, 4, HEADS, 8, 128)[:4].transpose(0, 3, 1, 2, 4)
    weight_grads = total.reshape(WIDTH, 4, HEADS, HEAD_DIM).astype(f32)
    return attention, token_grads, weight_grads


def solution(mesh):
    inner = Mesh(mesh.devices.reshape(SIZES), AXES)
    strips = P(("zl", "x"), ("zh", "y", "c"), None, None)
    rows = P(("zh", "y", "c"), None, None, None)
    return jax.shard_map(
        work,
        mesh=inner,
        in_specs=(strips, strips, rows),
        out_specs=(strips, strips, rows),
        check_vma=False,
    )
```
